256 devices in a mesh: illum: 32 (over z_hi, x, y), row: 8 (over z_lo, core).
Axes of the slice: x: 4, y: 4, z: 8 (z_hi: 2, z_lo: 4; z = z_hi * 4 + z_lo), core: 2. Of those that a mesh axis runs over, the one named last changes fastest.
Arguments:
- angles: int32 [128, 2], P('illum'), may hold values from -8 to 8
- depth_order: int32 [3], replicated, may hold values from 0 to 31, as said below
- slices: float32 [32, 64, 4096], P('illum', 'row'), may hold values from -4 to 4
- cotangent: float32 [128, 2, 64, 4096], P('illum', None, 'row'), may hold values from -0.6 to 0.6
Outputs:
- exit_field: float32 [128, 2, 64, 4096], P('illum', None, 'row')
- slice_grad: float32 [32, 64, 4096], P('illum', 'row')
The draws below stay inside these ranges and needn't reach their ends.
Inputs may be any that keep to these rules, and one draw needn't show every extreme that they name: `depth_order`: 3 distinct slice numbers; slice 0 and the last slice are always among them.
All inputs are finite; a program needn't handle non-finite values.
Results may differ from the reference program's by a relative error of at most 0.0001.
Values sent between devices are 32-bit elements; how exact they have to be, the bound alone decides.
No kernel may reach another device: no remote copies, remote signals or barrier semaphores. Data moves between devices by JAX's collectives and lax.ppermute only.
A program may use at most 64 MiB of HBM per device.

```python
import math
import jax
import jax.numpy as jnp

NY = 4096
LAYERS = 3
NX = 64
ILLUMS = 128
SLICES = 32
N_ILLUM = 32


def draw_depth_order(key, part):
    first_key = jax.random.fold_in(key, 11)
    second_key = jax.random.fold_in(key, 23)
    middle = 1 + jax.random.permutation(first_key, SLICES - 2)[:LAYERS - 2].astype(jnp.int32)
    values = jnp.concatenate([jnp.zeros((1,), jnp.int32), middle, jnp.full((1,), SLICES - 1, jnp.int32)])
    order = jax.random.permutation(second_key, LAYERS)
    return values[order].astype(jnp.int32)


def place_ends(drawn, own_key, low, largest):
    extent = drawn.shape
    index_at = [jax.random.randint(jax.random.fold_in(own_key, axis), (), 0, extent[axis]) for axis in range(len(extent))]
    drawn = drawn.at[tuple(index_at)].set(low)
    longest = extent.index(max(extent))
    index_at[longest] = (index_at[longest] + 1) % extent[longest]
    return drawn.at[tuple(index_at)].set(largest)


def levels(own_key, extent, split, low, top_value):
    def one(axis_at, shards_of):
        draws = jax.random.uniform(jax.random.fold_in(jax.random.fold_in(own_key, 6), axis_at), (shards_of,), jnp.float32, low / len(split), top_value / len(split))
        return jnp.repeat(jnp.exp(draws), extent[axis_at] // shards_of).reshape((-1,) + (1,) * (len(extent) - axis_at - 1))

    level = one(*split[0])
    for cut in split[1:]:
        level = level * one(*cut)
    return level


def normal_values(own_key, extent, deviation, reach, split=(), held_as=jnp.bfloat16):
    level = levels(own_key, extent, split, -0.22, 0.18) if split else 1.0
    entries = jax.random.normal(own_key, extent, jnp.float32) * deviation * level
    return jnp.minimum(jnp.maximum(entries, -reach), reach).astype(held_as)


def setup_inputs(seed: int = 0) -> dict:
    seeds = jax.random.split(jax.random.key(seed), 5)
    angles = place_ends(jax.random.randint(seeds[0], (ILLUMS, 2), -8, 9), jax.random.fold_in(seeds[0], 1), -8, 8).astype(jnp.int32)
    depth_order = draw_depth_order(jax.random.fold_in(seeds[4], 71), 0)
    slices = normal_values(seeds[2], (SLICES, NX, NY), 1.0, 4.0, ((0, 32), (1, 8)), jnp.float32)
    cotangent = normal_values(seeds[3], (ILLUMS, 2, NX, NY), 0.1, 0.6, ((0, 32), (2, 8)), jnp.float32)
    return dict(angles=angles, depth_order=depth_order, slices=slices, cotangent=cotangent)


rate_scale = 0.3


def laplace(field):
    padded = jnp.pad(field, [(0, 0)] * (field.ndim - 2) + [(1, 1), (1, 1)])
    return (padded[..., 2:, 1:-1] + padded[..., :-2, 1:-1]) + (padded[..., 1:-1, 2:] + padded[..., 1:-1, :-2]) - 4.0 * field


def rate(field, factor):
    curved = laplace(field)
    return jnp.stack([-factor * curved[:, 1], factor * curved[:, 0]], axis=1)


def runge_step(field, factor):
    slope_one = rate(field, factor)
    slope_two = rate(field + 0.5 * slope_one, factor)
    slope_three = rate(field + 0.5 * slope_two, factor)
    slope_four = rate(field + slope_three, factor)
    return field + (slope_one + 2.0 * slope_two + 2.0 * slope_three + slope_four) / 6.0


def rotate(field, phase):
    cosine = jnp.cos(phase)
    sine = jnp.sin(phase)
    real_part = field[:, 0]
    imag_part = field[:, 1]
    return jnp.stack([cosine * real_part - sine * imag_part, sine * real_part + cosine * imag_part], axis=1)


def reference(angles, depth_order, slices, cotangent):
    rows_idx = jnp.arange(NX, dtype=jnp.int32)
    cols_idx = jnp.arange(NY, dtype=jnp.int32)
    phase_rows = 2.0 * math.pi * ((angles[:, 0:1] * rows_idx[None, :]) % NX).astype(jnp.float32) / NX
    phase_cols = 2.0 * math.pi * ((angles[:, 1:2] * cols_idx[None, :]) % NY).astype(jnp.float32) / NY
    phase = phase_rows[:, :, None] + phase_cols[:, None, :]
    field = jnp.stack([jnp.cos(phase), jnp.sin(phase)], axis=1)
    kept = []
    chosen = []
    for layer in range(LAYERS):
        plane = slices[depth_order[layer]]
        chosen.append(plane)
        field = rotate(field, plane)
        kept.append(field)
        field = runge_step(field, rate_scale)
    exit_field = field
    adjoint = cotangent
    owners = jnp.arange(N_ILLUM, dtype=jnp.int32)
    slice_grad = jnp.zeros((N_ILLUM, NX, NY), jnp.float32)
    for layer in range(LAYERS - 1, -1, -1):
        adjoint = runge_step(adjoint, -rate_scale)
        stored = kept[layer]
        term = jnp.sum(-adjoint[:, 0] * stored[:, 1] + adjoint[:, 1] * stored[:, 0], axis=0)
        picked = (owners == depth_order[layer]).astype(jnp.float32)
        slice_grad = slice_grad + picked[:, None, None] * term[None]
        adjoint = rotate(adjoint, -chosen[layer])
    return exit_field, slice_grad
```

```python
import functools
import math

import jax
import jax.numpy as jnp
from jax import lax
from jax.experimental import pallas as pl
from jax.experimental.pallas import tpu as pltpu
from jax.sharding import PartitionSpec as P

rate_scale = 0.3
ROWS = 8
COLS = 4096
TILES = COLS // 128
LAYERS = 3
HALO = 8
EXT = ROWS + 2 * HALO

SIN_C = (0.9999999996397458, -0.16666666036106006, 0.00833331543673961,
         -0.00019839409893936808, 2.7469726872825416e-06, -2.3138942785856126e-08)
COS_C = (0.9999999953627682, -0.49999991881071015, 0.04166643614419552,
         -0.001388649171259302, 2.4688583708756773e-05, -2.5084304017242627e-07)


def horner(coefs, z):
    r = z * coefs[-1] + coefs[-2]
    for c in coefs[-3::-1]:
        r = r * z + c
    return r


def sincos(x):
    y = x * 0.5
    z = y * y
    s = y * horner(SIN_C, z)
    c = horner(COS_C, z)
    s2 = s + s
    return s2 * c, 1.0 - s2 * s


def cs(t):
    return slice(t * 128, (t + 1) * 128)


class Masks:
    def __init__(self):
        lane = lax.broadcasted_iota(jnp.int32, (8, 128), 1)
        sub = lax.broadcasted_iota(jnp.int32, (8, 128), 0)
        self.first = lane == 0
        self.last = lane == 127
        self.even = (sub & 1) == 0

    def turn(self, x):
        return jnp.where(self.even, -pltpu.roll(x, 7, 0), pltpu.roll(x, 1, 0))


def lap_tiles(m, src, r):
    c = [src[r, :, cs(t)] for t in range(TILES)]
    rl = [pltpu.roll(v, 1, 1) for v in c]
    rr = [pltpu.roll(v, 127, 1) for v in c]
    zero = jnp.zeros((8, 128), jnp.float32)
    out = []
    for t in range(TILES):
        left = jnp.where(m.first, rl[t - 1] if t else zero, rl[t])
        right = jnp.where(m.last, rr[t + 1] if t < TILES - 1 else zero, rr[t])
        out.append((src[r - 1, :, cs(t)] + src[r + 1, :, cs(t)]) + (left + right) - 4.0 * c[t])
    return out


def clear_edges(row, ref, base):
    @pl.when(row == 0)
    def _():
        ref[base - 1] = jnp.zeros((8, COLS), jnp.float32)

    @pl.when(row == 7)
    def _():
        ref[base + ROWS] = jnp.zeros((8, COLS), jnp.float32)


def step(m, row, src, base, h, powers, factor, write, edge_write=None):
    prev = src
    for k, dst in enumerate(powers):
        lo, hi = base - h + 1 + k, base + ROWS + h - 1 - k

        def body(r, _, prev=prev, dst=dst):
            for t, v in enumerate(lap_tiles(m, prev, r)):
                dst[r, :, cs(t)] = v
            return 0

        lax.fori_loop(lo, hi, body, 0)
        clear_edges(row, dst, base)
        prev = dst
    l1, l2, l3 = powers
    c1, c2, c3, c4 = factor, -factor**2 / 2, -factor**3 / 6, factor**4 / 24

    def last(r, _, put):
        for t, v4 in enumerate(lap_tiles(m, l3, r)):
            even = src[r, :, cs(t)] + (c2 * l2[r, :, cs(t)] + c4 * v4)
            odd = c1 * l1[r, :, cs(t)] + c3 * l3[r, :, cs(t)]
            put(r, t, even + m.turn(odd))
        return 0

    lo, hi = base - h + 4, base + ROWS + h - 4
    if edge_write is None:
        lax.fori_loop(lo, hi, functools.partial(last, put=write), 0)
    else:
        lax.fori_loop(base, base + ROWS, functools.partial(last, put=write), 0)
        lax.fori_loop(lo, base, functools.partial(last, put=edge_write), 0)
        lax.fori_loop(base + ROWS, hi, functools.partial(last, put=edge_write), 0)


def planes(r, t):
    return pl.ds(t * ROWS + r, 8, stride=TILES * ROWS)


def split_kernel(cot, low, high):
    for r in range(4):
        for t in range(TILES):
            low[r, :, cs(t)] = cot[planes(r, t), :]
            high[r, :, cs(t)] = cot[planes(r + 4, t), :]


def adjoint_kernel(row_ref, cot, top, bot, out, u, l1, l2, l3):
    m = Masks()
    row = row_ref[0]
    for r in range(4):
        u[r] = top[r]
        u[12 + r] = bot[r]
    for r in range(ROWS):
        for t in range(TILES):
            u[4 + r, :, cs(t)] = cot[planes(r, t), :]

    def write(r, t, v):
        out[r - 4, :, cs(t)] = v

    step(m, row, u, 4, 4, (l1, l2, l3), -rate_scale, write)


def exit_kernel(row_ref, own, top, bot, out, u, l1, l2, l3):
    m = Masks()
    row = row_ref[0]
    for r in range(4):
        u[r] = top[r]
        u[12 + r] = bot[r]
    for r in range(ROWS):
        u[4 + r] = own[r]

    def write(r, t, v):
        out[planes(r - 4, t), :] = v

    step(m, row, u, 4, 4, (l1, l2, l3), rate_scale, write)


def main_kernel(row_ref, p8, q8, phases, w_own, w_top, w_bot, terms, last_refr,
                cosr, sinr, beam, beam_turn, u, v, w, w2, l1, l2, l3):
    m = Masks()
    row = row_ref[0]

    def trig(t, _):
        for j in range(LAYERS * EXT // 8):
            s, c = sincos(phases[t, j * 8:(j + 1) * 8, :])
            sinr[t, j * 8:(j + 1) * 8, :] = s
            cosr[t, j * 8:(j + 1) * 8, :] = c
        k = (q8[...] * (t * 128 + lax.broadcasted_iota(jnp.int32, (8, 128), 1))) & (COLS - 1)
        s, c = sincos((k - COLS // 2).astype(jnp.float32) * (2.0 * math.pi / COLS))
        at = pl.ds(pl.multiple_of(t * 128, 128), 128)
        beam[:, at] = jnp.where(m.even, -c, -s)
        beam_turn[:, at] = jnp.where(m.even, s, -c)
        return 0

    lax.fori_loop(0, TILES, trig, 0)

    def phase_at(layer, r, t):
        at = pl.ds(layer * EXT + r, 1)
        c = jnp.broadcast_to(cosr[t, at, :], (8, 128))
        s = jnp.broadcast_to(sinr[t, at, :], (8, 128))
        return c, s

    total = 8 * ROWS

    def incident(r, _):
        k = (p8[...] * (row * ROWS + r - HALO)) & (total - 1)
        sa, ca = sincos((k - total // 2).astype(jnp.float32) * (2.0 * math.pi / total))
        for t in range(TILES):
            c, s = phase_at(0, r, t)
            u[r, :, cs(t)] = (beam_turn[:, cs(t)] * -(sa * c + ca * s)
                              - beam[:, cs(t)] * (ca * c - sa * s))
        return 0

    lax.fori_loop(0, EXT, incident, 0)
    clear_edges(row, u, HALO)

    def write_v(r, t, x):
        c, s = phase_at(1, r, t)
        v[r, :, cs(t)] = x * c + m.turn(x) * s

    step(m, row, u, HALO, 8, (l1, l2, l3), rate_scale, write_v)
    clear_edges(row, v, HALO)

    def write_last(r, t, x):
        c, s = phase_at(2, r, t)
        last_refr[r - HALO, :, cs(t)] = x * c + m.turn(x) * s

    step(m, row, v, HALO, 4, (l1, l2, l3), rate_scale, write_last)

    def term(layer, r, t, adjoint, stored):
        terms[t, pl.ds(layer * ROWS + r, 1), :] = jnp.sum(
            adjoint * m.turn(stored), axis=0, keepdims=True)

    def term_two(r, _):
        for t in range(TILES):
            term(2, r, t, w_own[r, :, cs(t)], last_refr[r, :, cs(t)])
        return 0

    lax.fori_loop(0, ROWS, term_two, 0)

    def back(src, first):
        def body(r, _):
            for t in range(TILES):
                c, s = phase_at(2, r + first, t)
                x = src[r, :, cs(t)]
                w[r + first, :, cs(t)] = x * c - m.turn(x) * s
            return 0

        lax.fori_loop(0, ROWS, body, 0)

    back(w_top, 0)
    back(w_own, HALO)
    back(w_bot, HALO + ROWS)

    def mid_edge(r, t, x):
        c, s = phase_at(1, r, t)
        w2[r, :, cs(t)] = x * c - m.turn(x) * s

    def mid(r, t, x):
        mid_edge(r, t, x)
        term(1, r - HALO, t, x, v[r, :, cs(t)])

    step(m, row, w, HALO, 8, (l1, l2, l3), -rate_scale, mid, mid_edge)
    clear_edges(row, w2, HALO)

    def final(r, t, x):
        term(0, r - HALO, t, x, u[r, :, cs(t)])

    step(m, row, w2, HALO, 4, (l1, l2, l3), -rate_scale, final)


def vm():
    return pl.BlockSpec(memory_space=pltpu.VMEM)


def sm():
    return pl.BlockSpec(memory_space=pltpu.SMEM)


def field(rows):
    return jax.ShapeDtypeStruct((rows, 8, COLS), jnp.float32)


def scratch(rows, n):
    return [pltpu.VMEM((rows, 8, COLS), jnp.float32)] * n


def call(kernel, ins, outs, scr, name, mib):
    return pl.pallas_call(
        kernel, out_shape=outs, in_specs=ins, out_specs=jax.tree.map(lambda _: vm(), outs),
        scratch_shapes=scr, name=name,
        compiler_params=pltpu.CompilerParams(vmem_limit_bytes=mib << 20),
        cost_estimate=pl.CostEstimate(flops=20_000_000, bytes_accessed=4 << 20, transcendentals=0),
    )


def body(angles, depth_order, slices, cotangent):
    peers = lax.axis_size("illum")
    n_row = lax.axis_size("row")
    row = lax.axis_index("row").astype(jnp.int32).reshape(1)
    me = lax.axis_index("illum")
    up = [(i, i + 1) for i in range(n_row - 1)]
    down = [(i + 1, i) for i in range(n_row - 1)]

    cot = cotangent.reshape(8, ROWS, TILES, 128).transpose(0, 2, 1, 3).reshape(-1, 128)
    low, high = call(split_kernel, [vm()], (field(4), field(4)), [], "split", 6)(cot)
    cot_top = lax.ppermute(high, "row", up)
    cot_bot = lax.ppermute(low, "row", down)

    mine = slices[0].reshape(ROWS, TILES, 128).transpose(1, 0, 2)
    got = lax.all_to_all(mine, "illum", 0, 0, tiled=True)
    chunk = jnp.concatenate(
        [lax.dynamic_slice_in_dim(got, depth_order[l], 1, 0) for l in range(LAYERS)], 0)

    w1 = call(adjoint_kernel, [sm(), vm(), vm(), vm()], field(8), scratch(16, 4), "adjoint1", 14)(
        row, cot, cot_top, cot_bot)
    w_top = lax.ppermute(w1, "row", up)
    w_bot = lax.ppermute(w1, "row", down)

    c_top = lax.ppermute(chunk, "row", up)
    c_bot = lax.ppermute(chunk, "row", down)
    wide = jnp.concatenate([c_top, chunk, c_bot], axis=1).reshape(LAYERS * EXT, 128)
    phases = lax.all_to_all(
        jnp.broadcast_to(wide[None], (peers, LAYERS * EXT, 128)), "illum", 0, 0, tiled=True)

    p8 = jnp.broadcast_to(jnp.repeat(angles[:, 0], 2)[:, None], (8, 128))
    q8 = jnp.broadcast_to(jnp.repeat(angles[:, 1], 2)[:, None], (8, 128))
    table = pltpu.VMEM((TILES, LAYERS * EXT, 128), jnp.float32)
    line = pltpu.VMEM((8, COLS), jnp.float32)
    terms, refr = call(
        main_kernel, [sm()] + [vm()] * 6,
        (jax.ShapeDtypeStruct((TILES, LAYERS * ROWS, 128), jnp.float32), field(8)),
        [table, table, line, line] + scratch(EXT, 7), "main", 36)(
            row, p8, q8, phases, w1, w_top, w_bot)
    r_top = lax.ppermute(refr[4:], "row", up)
    r_bot = lax.ppermute(refr[:4], "row", down)

    parts = lax.all_to_all(terms, "illum", 0, 0, tiled=True)
    summed = jnp.sum(parts, axis=0).reshape(LAYERS, ROWS, 128)
    owners = jnp.arange(peers, dtype=jnp.int32)
    send = sum(
        jnp.where((owners == depth_order[l])[:, None, None], summed[l][None], 0.0)
        for l in range(LAYERS))
    out = call(exit_kernel, [sm(), vm(), vm(), vm()],
               jax.ShapeDtypeStruct(cot.shape, jnp.float32),
               scratch(16, 4), "exit", 14)(row, refr, r_top, r_bot)
    grad = lax.all_to_all(send, "illum", 0, 0, tiled=True)
    grad = grad.transpose(1, 0, 2).reshape(1, ROWS, COLS)
    out = out.reshape(8, TILES, ROWS, 128).transpose(0, 2, 1, 3)
    return out.reshape(cotangent.shape), grad


def solution(mesh):
    placed = (P("illum", None), P(), P("illum", "row", None), P("illum", None, "row", None))
    return jax.shard_map(
        body,
        mesh=mesh,
        in_specs=placed,
        out_specs=(P("illum", None, "row", None), P("illum", "row", None)),
        check_vma=False,
    )
```

```python
import functools
import math

import jax
import jax.numpy as jnp
from jax import lax
from jax.experimental import pallas as pl
from jax.experimental.pallas import tpu as pltpu
from jax.sharding import PartitionSpec as P

rate_scale = 0.3
ROWS = 8
COLS = 4096
TILES = COLS // 128
LAYERS = 3
HALO = 8
EXT = ROWS + 2 * HALO
N_ROW = 8
NX = ROWS * N_ROW
PAD = 144
PLANE = 16

SIN_C = (0.9999999996397458, -0.16666666036106006, 0.00833331543673961,
         -0.00019839409893936808, 2.7469726872825416e-06, -2.3138942785856126e-08)
COS_C = (0.9999999953627682, -0.49999991881071015, 0.04166643614419552,
         -0.001388649171259302, 2.4688583708756773e-05, -2.5084304017242627e-07)


def horner(coefs, z):
    r = z * coefs[-1] + coefs[-2]
    for c in coefs[-3::-1]:
        r = r * z + c
    return r


def sincos(x):
    y = x * 0.5
    z = y * y
    s = y * horner(SIN_C, z)
    c = horner(COS_C, z)
    s2 = s + s
    return s2 * c, 1.0 - s2 * s


def chunk(j):
    return slice(8 * j, 8 * j + 8)


def padded(j, shift=0):
    return slice(8 + 8 * j + shift, 16 + 8 * j + shift)


def fill_pads(ref, rows):
    flat = ref.reshape(rows * 2 * PAD, 128)
    tile = lax.broadcasted_iota(jnp.int32, (rows * 2, 128), 1) & (TILES - 1)
    high = flat[pl.ds(135, rows * 2, stride=PAD), :]
    low = flat[pl.ds(8, rows * 2, stride=PAD), :]
    flat[pl.ds(7, rows * 2, stride=PAD), :] = jnp.where(tile == 0, 0.0, pltpu.roll(high, 1, 1))
    flat[pl.ds(136, rows * 2, stride=PAD), :] = jnp.where(
        tile == TILES - 1, 0.0, pltpu.roll(low, 127, 1))


def clear_outside(row, ref, base, rows):
    for at in (base - 1 - ROWS * row, base + NX - ROWS * row):
        @pl.when((at >= 0) & (at < rows))
        def _(at=at):
            ref[at] = jnp.zeros((2, PAD, 128), jnp.float32)


def lap_pair(src, r, k, j):
    v = [src[r + q, k, padded(j), :] for q in (-1, 0, 1, 2)]
    out = []
    for q in (0, 1):
        side = src[r + q, k, padded(j, -1), :] + src[r + q, k, padded(j, 1), :]
        out.append((v[q] + v[q + 2]) + side - 4.0 * v[q + 1])
    return out


def step(row, src, rows, base, h, powers, factor, write):
    prev = src
    for n, dst in enumerate(powers):
        lo, count = base - h + 1 + n, ROWS + 2 * (h - 1 - n)

        def body(i, _, prev=prev, dst=dst, lo=lo):
            r = lo + 2 * i
            for k in range(2):
                for j in range(16):
                    a, b = lap_pair(prev, r, k, j)
                    dst[r, k, padded(j), :] = a
                    dst[r + 1, k, padded(j), :] = b
            return 0

        lax.fori_loop(0, count // 2, body, 0)
        fill_pads(dst, rows)
        clear_outside(row, dst, base, rows)
        prev = dst
    l1, l2, l3 = powers
    c1, c2, c3, c4 = factor, -factor**2 / 2, -factor**3 / 6, factor**4 / 24
    lo = base - h + 4

    def last(i, _):
        r = lo + 2 * i
        for j in range(16):
            l4 = [lap_pair(l3, r, k, j) for k in range(2)]
            for q in (0, 1):
                even, odd = [], []
                for k in range(2):
                    at = (r + q, k, padded(j), slice(None))
                    even.append(src[at] + (c2 * l2[at] + c4 * l4[k][q]))
                    odd.append(c1 * l1[at] + c3 * l3[at])
                write(r + q, j, even[0] - odd[1], even[1] + odd[0])
        return 0

    lax.fori_loop(0, (ROWS + 2 * (h - 4)) // 2, last, 0)


def natural(g, k, r):
    return pl.ds((g * 2 + k) * TILES * ROWS + r, TILES, stride=ROWS)


def split_kernel(cot, out, low, high):
    def body(r, _):
        for k in range(2):
            out[r, k] = jnp.concatenate([cot[natural(g, k, r), :] for g in range(4)], axis=0).T
        return 0

    lax.fori_loop(0, ROWS, body, 0)
    for r in range(4):
        low[r] = out[r]
        high[r] = out[r + 4]


def put(dst, at, src, n):
    def body(r, _):
        for k in range(2):
            dst[at + r, k, 8:136, :] = src[r, k]
        return 0

    lax.fori_loop(0, n, body, 0)


def adjoint_kernel(row_ref, own, top, bot, top2, bot2, out, u, l1, l2, l3):
    row = row_ref[0]
    put(u, 0, top2, 4)
    put(u, 4, top, 8)
    put(u, 12, own, 8)
    put(u, 20, bot, 8)
    put(u, 28, bot2, 4)
    fill_pads(u, 32)

    def write(r, j, re, im):
        out[r - 4, 0, chunk(j), :] = re
        out[r - 4, 1, chunk(j), :] = im

    step(row, u, 32, 12, 12, (l1, l2, l3), -rate_scale, write)


def exit_kernel(row_ref, low, high, top, bot, out, u, l1, l2, l3, res):
    row = row_ref[0]
    put(u, 0, top, 4)
    put(u, 4, low, 4)
    put(u, 8, high, 4)
    put(u, 12, bot, 4)
    fill_pads(u, 16)

    def write(r, j, re, im):
        res[r - 4, 0, chunk(j), :] = re
        res[r - 4, 1, chunk(j), :] = im

    step(row, u, 16, 4, 4, (l1, l2, l3), rate_scale, write)

    def body(r, _):
        for k in range(2):
            x = res[r, k].T
            for g in range(4):
                out[natural(g, k, r), :] = x[g * TILES:(g + 1) * TILES]
        return 0

    lax.fori_loop(0, ROWS, body, 0)


def trig_tables(phases, cos_n, sin_n):
    def body(i, _):
        at = pl.ds(pl.multiple_of(i * 24, 8), 24)
        s, c = sincos(phases[at, :])
        sin_n[at, :] = s
        cos_n[at, :] = c
        return 0

    lax.fori_loop(0, TILES, body, 0)


def spread(ref, n):
    x = ref[pl.ds(n, TILES, stride=LAYERS * ROWS), :]
    return jnp.concatenate([x] * 4, axis=0).T


def phase_kernel(phases, cos_out, sin_out, cos_n, sin_n):
    trig_tables(phases, cos_n, sin_n)

    def body(n, _):
        cos_out[n] = spread(cos_n, n)
        sin_out[n] = spread(sin_n, n)
        return 0

    lax.fori_loop(0, LAYERS * ROWS, body, 0)


def main_kernel(row_ref, pv, qv, ph_top, ph_bot, cos_own, sin_own, w1,
                terms, last_low, last_high,
                cos_n, sin_n, cosr, sinr, beam, u, v, w, w2, raw, l1, l2, l3):
    row = row_ref[0]
    for ph, first in ((ph_top, 0), (ph_bot, HALO + ROWS)):
        trig_tables(ph, cos_n, sin_n)
        for layer in range(LAYERS):
            lo, hi = (0, 8) if layer != 1 else ((4, 8) if first == 0 else (0, 4))

            def body(r, _, layer=layer, first=first):
                cosr[layer * EXT + first + r] = spread(cos_n, layer * ROWS + r)
                sinr[layer * EXT + first + r] = spread(sin_n, layer * ROWS + r)
                return 0

            lax.fori_loop(lo, hi, body, 0)
    for layer in range(LAYERS):
        def copy(r, _, layer=layer):
            cosr[layer * EXT + HALO + r] = cos_own[layer * ROWS + r]
            sinr[layer * EXT + HALO + r] = sin_own[layer * ROWS + r]
            return 0

        lax.fori_loop(0, ROWS, copy, 0)

    lane = lax.broadcasted_iota(jnp.int32, (8, 128), 1)
    sub = lax.broadcasted_iota(jnp.int32, (8, 128), 0)
    for j in range(16):
        col = (lane & (TILES - 1)) * 128 + sub + 8 * j
        k = (qv[...] * col) & (COLS - 1)
        s, c = sincos((k - COLS // 2).astype(jnp.float32) * (2.0 * math.pi / COLS))
        beam[0, chunk(j), :] = -c
        beam[1, chunk(j), :] = -s

    def phase_at(layer, r, j):
        return cosr[layer * EXT + r, chunk(j), :], sinr[layer * EXT + r, chunk(j), :]

    def incident(r, _):
        k = (pv[...] * (row * ROWS + r - HALO)) & (NX - 1)
        sa, ca = sincos((k - NX // 2).astype(jnp.float32) * (2.0 * math.pi / NX))
        for j in range(16):
            c, s = phase_at(0, r, j)
            a = sa * s - ca * c
            b = -(sa * c + ca * s)
            er, ei = beam[0, chunk(j), :], beam[1, chunk(j), :]
            u[r, 0, padded(j), :] = er * a - ei * b
            u[r, 1, padded(j), :] = ei * a + er * b
        return 0

    lax.fori_loop(0, EXT, incident, 0)
    fill_pads(u, EXT)
    clear_outside(row, u, HALO, EXT)

    def write_v(r, j, re, im):
        c, s = phase_at(1, r, j)
        v[r, 0, padded(j), :] = re * c - im * s
        v[r, 1, padded(j), :] = re * s + im * c

    step(row, u, EXT, HALO, 8, (l1, l2, l3), rate_scale, write_v)
    fill_pads(v, EXT)
    clear_outside(row, v, HALO, EXT)

    def write_last(r, j, re, im):
        c, s = phase_at(2, r, j)
        w2[r, 0, padded(j), :] = re * c - im * s
        w2[r, 1, padded(j), :] = re * s + im * c

    step(row, v, EXT, HALO, 4, (l1, l2, l3), rate_scale, write_last)
    for r in range(4):
        for k in range(2):
            last_low[r, k] = w2[HALO + r, k, 8:136, :]
            last_high[r, k] = w2[HALO + 4 + r, k, 8:136, :]

    def term(layer, adjoint, stored):
        def body(r, _):
            x = adjoint(r, 1) * stored(r, 0) - adjoint(r, 0) * stored(r, 1)
            x = x.T
            x = (x[:TILES] + x[TILES:2 * TILES]) + (x[2 * TILES:3 * TILES] + x[3 * TILES:])
            terms[pl.ds(layer * ROWS + r, TILES, stride=LAYERS * ROWS), :] = x
            return 0

        lax.fori_loop(0, ROWS, body, 0)

    def own(ref):
        return lambda r, k: ref[HALO + r, k, 8:136, :]

    term(2, lambda r, k: w1[HALO + r, k], own(w2))

    def back(r, _):
        for j in range(16):
            c, s = phase_at(2, r, j)
            re, im = w1[r, 0, chunk(j), :], w1[r, 1, chunk(j), :]
            w[r, 0, padded(j), :] = re * c + im * s
            w[r, 1, padded(j), :] = im * c - re * s
        return 0

    lax.fori_loop(0, EXT, back, 0)
    fill_pads(w, EXT)
    clear_outside(row, w, HALO, EXT)

    def mid(r, j, re, im):
        c, s = phase_at(1, r, j)
        raw[r - 4, 0, chunk(j), :] = re
        raw[r - 4, 1, chunk(j), :] = im
        w2[r, 0, padded(j), :] = re * c + im * s
        w2[r, 1, padded(j), :] = im * c - re * s

    step(row, w, EXT, HALO, 8, (l1, l2, l3), -rate_scale, mid)
    fill_pads(w2, EXT)
    clear_outside(row, w2, HALO, EXT)
    term(1, lambda r, k: raw[r + 4, k], own(v))

    def final(r, j, re, im):
        raw[r - 4, 0, chunk(j), :] = re
        raw[r - 4, 1, chunk(j), :] = im

    step(row, w2, EXT, HALO, 4, (l1, l2, l3), -rate_scale, final)
    term(0, lambda r, k: raw[r + 4, k], own(u))


def vm():
    return pl.BlockSpec(memory_space=pltpu.VMEM)


def sm():
    return pl.BlockSpec(memory_space=pltpu.SMEM)


def shape(*dims):
    return jax.ShapeDtypeStruct(dims, jnp.float32)


def field(rows):
    return shape(rows, 2, 128, 128)


def scr(*dims):
    return pltpu.VMEM(dims, jnp.float32)


def wide(rows):
    return scr(rows, 2, PAD, 128)


def call(kernel, ins, outs, scratch, name, mib):
    return pl.pallas_call(
        kernel, out_shape=outs, in_specs=ins, out_specs=jax.tree.map(lambda _: vm(), outs),
        scratch_shapes=scratch, name=name,
        compiler_params=pltpu.CompilerParams(vmem_limit_bytes=mib << 20),
        cost_estimate=pl.CostEstimate(flops=20_000_000, bytes_accessed=4 << 20, transcendentals=0),
    )


def body(angles, depth_order, slices, cotangent):
    row = lax.axis_index("row").astype(jnp.int32).reshape(1)
    z = lax.axis_index("illum") // PLANE
    here = lax.axis_index("illum") % PLANE
    n_row = lax.axis_size("row")
    groups = [list(range(g * PLANE, (g + 1) * PLANE)) for g in range(2)]
    swap = [(i, (i + PLANE) % (2 * PLANE)) for i in range(2 * PLANE)]

    def to_next(x, by):
        return lax.ppermute(x, "row", [(i, i + by) for i in range(n_row - by)])

    def to_prev(x, by):
        return lax.ppermute(x, "row", [(i + by, i) for i in range(n_row - by)])

    def exchange(x):
        return lax.all_to_all(x, "illum", 0, 0, axis_index_groups=groups, tiled=True)

    mine = slices[0]
    other = lax.ppermute(mine, "illum", swap)

    cot = cotangent.reshape(8, ROWS, TILES, 128).transpose(0, 2, 1, 3).reshape(-1, 128)
    own, low, high = call(split_kernel, [vm()], (field(8), field(4), field(4)), [], "split", 8)(cot)
    top, bot = to_next(own, 1), to_prev(own, 1)
    top2, bot2 = to_next(high, 2), to_prev(low, 2)

    both = jnp.stack([jnp.where(z == 0, mine, other), jnp.where(z == 0, other, mine)], 0)
    both = both.reshape(2 * ROWS, TILES, 128).transpose(1, 0, 2)
    got = exchange(both.reshape(TILES * 2 * ROWS, 128)).reshape(PLANE, 2, 2, ROWS, 128)
    picked = [
        lax.dynamic_slice(got, (depth_order[l] % PLANE, 0, depth_order[l] // PLANE, 0, 0),
                          (1, 2, 1, ROWS, 128))[0]
        for l in range(LAYERS)
    ]
    piece = jnp.concatenate(picked, 1).reshape(1, 2 * LAYERS * ROWS, 128)
    phases = exchange(
        jnp.broadcast_to(piece, (PLANE, 2 * LAYERS * ROWS, 128)).reshape(-1, 128))
    ph_top, ph_bot = to_next(phases, 1), to_prev(phases, 1)

    w1 = call(adjoint_kernel, [sm()] + [vm()] * 5, field(EXT), [wide(32)] * 4, "adjoint1", 26)(
        row, own, top, bot, top2, bot2)
    table = scr(TILES * LAYERS * ROWS, 128)
    cos_own, sin_own = call(
        phase_kernel, [vm()], (shape(LAYERS * ROWS, 128, 128),) * 2, [table] * 2, "phases", 8)(
            phases)

    pv = jnp.broadcast_to(jnp.repeat(angles[:, 0], TILES)[None], (8, 128))
    qv = jnp.broadcast_to(jnp.repeat(angles[:, 1], TILES)[None], (8, 128))
    spreads = scr(LAYERS * EXT, 128, 128)
    terms, last_low, last_high = call(
        main_kernel, [sm()] + [vm()] * 7,
        (shape(TILES * LAYERS * ROWS, 128), field(4), field(4)),
        [table, table, spreads, spreads, scr(2, 128, 128)] + [wide(EXT)] * 4
        + [scr(16, 2, 128, 128)] + [wide(EXT)] * 3, "main", 52)(
            row, pv, qv, ph_top, ph_bot, cos_own, sin_own, w1)
    r_top, r_bot = to_next(last_high, 1), to_prev(last_low, 1)

    parts = exchange(terms).reshape(PLANE, 2, LAYERS, ROWS, 128)
    half = jnp.sum(parts, axis=0)
    full = half + lax.ppermute(half, "illum", swap)
    owners = jnp.arange(PLANE, dtype=jnp.int32) + z * PLANE
    send = sum(
        jnp.where((owners == depth_order[l])[:, None, None, None], full[None, :, l], 0.0)
        for l in range(LAYERS))
    out = call(exit_kernel, [sm()] + [vm()] * 4, shape(2048, 128),
               [wide(16)] * 4 + [scr(8, 2, 128, 128)], "exit", 16)(
                   row, last_low, last_high, r_top, r_bot)
    grad = exchange(send.reshape(TILES * ROWS, 128)).reshape(TILES, ROWS, 128)
    grad = grad.transpose(1, 0, 2).reshape(1, ROWS, COLS)
    out = out.reshape(8, TILES, ROWS, 128).transpose(0, 2, 1, 3)
    return out.reshape(cotangent.shape), grad


def solution(mesh):
    placed = (P("illum", None), P(), P("illum", "row", None), P("illum", None, "row", None))
    return jax.shard_map(
        body,
        mesh=mesh,
        in_specs=placed,
        out_specs=(P("illum", None, "row", None), P("illum", "row", None)),
        check_vma=False,
    )
```

```python
import math

import jax
import jax.numpy as jnp
from jax import lax
from jax.experimental import pallas as pl
from jax.experimental.pallas import tpu as pltpu
from jax.sharding import PartitionSpec as P


rate_scale = 0.3
ROWS = 8
COLS = 4096
TILES = COLS // 128
LAYERS = 3
HALO = 8
EXT = ROWS + 2 * HALO
N_ROW = 8
NX = ROWS * N_ROW
PAD = 144
PLANE = 16

SIN_C = (0.9999999996397458, -0.16666666036106006, 0.00833331543673961,
         -0.00019839409893936808, 2.7469726872825416e-06, -2.3138942785856126e-08)
COS_C = (0.9999999953627682, -0.49999991881071015, 0.04166643614419552,
         -0.001388649171259302, 2.4688583708756773e-05, -2.5084304017242627e-07)


def horner(coefs, z):
    r = z * coefs[-1] + coefs[-2]
    for c in coefs[-3::-1]:
        r = r * z + c
    return r


def sincos(x):
    y = x * 0.5
    z = y * y
    s = y * horner(SIN_C, z)
    c = horner(COS_C, z)
    s2 = s + s
    return s2 * c, 1.0 - s2 * s


def chunk(j):
    return slice(8 * j, 8 * j + 8)


def padded(j, shift=0):
    return slice(8 + 8 * j + shift, 16 + 8 * j + shift)


def fill_pads(ref, rows):
    flat = ref.reshape(rows * 2 * PAD, 128)
    tile = lax.broadcasted_iota(jnp.int32, (rows * 2, 128), 1) & (TILES - 1)
    high = flat[pl.ds(135, rows * 2, stride=PAD), :]
    low = flat[pl.ds(8, rows * 2, stride=PAD), :]
    flat[pl.ds(7, rows * 2, stride=PAD), :] = jnp.where(tile == 0, 0.0, pltpu.roll(high, 1, 1))
    flat[pl.ds(136, rows * 2, stride=PAD), :] = jnp.where(
        tile == TILES - 1, 0.0, pltpu.roll(low, 127, 1))


def clear_outside(row, ref, base, rows):
    for at in (base - 1 - ROWS * row, base + NX - ROWS * row):
        @pl.when((at >= 0) & (at < rows))
        def _(at=at):
            ref[at] = jnp.zeros((2, PAD, 128), jnp.float32)


def lap_pair(src, r, k, j):
    v = [src[r + q, k, padded(j), :] for q in (-1, 0, 1, 2)]
    out = []
    for q in (0, 1):
        side = src[r + q, k, padded(j, -1), :] + src[r + q, k, padded(j, 1), :]
        out.append((v[q] + v[q + 2]) + side - 4.0 * v[q + 1])
    return out


def step(row, src, rows, base, h, powers, factor, write):
    prev = src
    for n, dst in enumerate(powers):
        lo, count = base - h + 1 + n, ROWS + 2 * (h - 1 - n)

        def body(i, _, prev=prev, dst=dst, lo=lo):
            r = lo + 2 * i
            for k in range(2):
                for j in range(16):
                    a, b = lap_pair(prev, r, k, j)
                    dst[r, k, padded(j), :] = a
                    dst[r + 1, k, padded(j), :] = b
            return 0

        lax.fori_loop(0, count // 2, body, 0)
        fill_pads(dst, rows)
        clear_outside(row, dst, base, rows)
        prev = dst
    l1, l2, l3 = powers
    c1, c2, c3, c4 = factor, -factor**2 / 2, -factor**3 / 6, factor**4 / 24
    lo = base - h + 4

    def last(i, _):
        r = lo + 2 * i
        for j in range(16):
            l4 = [lap_pair(l3, r, k, j) for k in range(2)]
            for q in (0, 1):
                even, odd = [], []
                for k in range(2):
                    at = (r + q, k, padded(j), slice(None))
                    even.append(src[at] + (c2 * l2[at] + c4 * l4[k][q]))
                    odd.append(c1 * l1[at] + c3 * l3[at])
                write(r + q, j, even[0] - odd[1], even[1] + odd[0])
        return 0

    lax.fori_loop(0, (ROWS + 2 * (h - 4)) // 2, last, 0)


def natural(g, k, r):
    return pl.ds((g * 2 + k) * TILES * ROWS + r, TILES, stride=ROWS)


def split_kernel(cot, out, low, high):
    def body(r, _):
        for k in range(2):
            out[r, k] = jnp.concatenate([cot[natural(g, k, r), :] for g in range(4)], axis=0).T
        return 0

    lax.fori_loop(0, ROWS, body, 0)
    for r in range(4):
        low[r] = out[r]
        high[r] = out[r + 4]


def put(dst, at, src, n):
    def body(r, _):
        for k in range(2):
            dst[at + r, k, 8:136, :] = src[r, k]
        return 0

    lax.fori_loop(0, n, body, 0)


def adjoint_kernel(row_ref, own, top, bot, top2, bot2, out, u, l1, l2, l3):
    row = row_ref[0]
    put(u, 0, top2, 4)
    put(u, 4, top, 8)
    put(u, 12, own, 8)
    put(u, 20, bot, 8)
    put(u, 28, bot2, 4)
    fill_pads(u, 32)

    def write(r, j, re, im):
        out[r - 4, 0, chunk(j), :] = re
        out[r - 4, 1, chunk(j), :] = im

    step(row, u, 32, 12, 12, (l1, l2, l3), -rate_scale, write)


def exit_kernel(row_ref, low, high, top, bot, out, u, l1, l2, l3, res):
    row = row_ref[0]
    put(u, 0, top, 4)
    put(u, 4, low, 4)
    put(u, 8, high, 4)
    put(u, 12, bot, 4)
    fill_pads(u, 16)

    def write(r, j, re, im):
        res[r - 4, 0, chunk(j), :] = re
        res[r - 4, 1, chunk(j), :] = im

    step(row, u, 16, 4, 4, (l1, l2, l3), rate_scale, write)

    def body(r, _):
        for k in range(2):
            x = res[r, k].T
            for g in range(4):
                out[natural(g, k, r), :] = x[g * TILES:(g + 1) * TILES]
        return 0

    lax.fori_loop(0, ROWS, body, 0)


def trig_tables(phases, cos_n, sin_n):
    def body(i, _):
        at = pl.ds(pl.multiple_of(i * 24, 8), 24)
        s, c = sincos(phases[at, :])
        sin_n[at, :] = s
        cos_n[at, :] = c
        return 0

    lax.fori_loop(0, TILES, body, 0)


def spread(ref, n):
    x = ref[pl.ds(n, TILES, stride=LAYERS * ROWS), :]
    return jnp.concatenate([x] * 4, axis=0).T


def phase_kernel(phases, cos_out, sin_out, cos_n, sin_n):
    trig_tables(phases, cos_n, sin_n)

    def body(i, _):
        for n in (2 * i, 2 * i + 1):
            cos_out[n] = spread(cos_n, n)
            sin_out[n] = spread(sin_n, n)
        return 0

    lax.fori_loop(0, LAYERS * ROWS // 2, body, 0)


def main_kernel(row_ref, pv, qv, ph_top, ph_bot, cos_own, sin_own, w1,
                terms, last_low, last_high,
                cos_n, sin_n, cosr, sinr, beam, u, v, w, w2, raw, l1, l2, l3):
    row = row_ref[0]
    for ph, first in ((ph_top, 0), (ph_bot, HALO + ROWS)):
        trig_tables(ph, cos_n, sin_n)
        for layer in range(LAYERS):
            lo, hi = (0, 8) if layer != 1 else ((4, 8) if first == 0 else (0, 4))

            def body(i, _, layer=layer, first=first, lo=lo):
                for r in (lo + 2 * i, lo + 2 * i + 1):
                    cosr[layer * EXT + first + r] = spread(cos_n, layer * ROWS + r)
                    sinr[layer * EXT + first + r] = spread(sin_n, layer * ROWS + r)
                return 0

            lax.fori_loop(0, (hi - lo) // 2, body, 0)
    for layer in range(LAYERS):
        def copy(r, _, layer=layer):
            cosr[layer * EXT + HALO + r] = cos_own[layer * ROWS + r]
            sinr[layer * EXT + HALO + r] = sin_own[layer * ROWS + r]
            return 0

        lax.fori_loop(0, ROWS, copy, 0)

    lane = lax.broadcasted_iota(jnp.int32, (8, 128), 1)
    sub = lax.broadcasted_iota(jnp.int32, (8, 128), 0)
    for j in range(16):
        col = (lane & (TILES - 1)) * 128 + sub + 8 * j
        k = (qv[...] * col) & (COLS - 1)
        s, c = sincos((k - COLS // 2).astype(jnp.float32) * (2.0 * math.pi / COLS))
        beam[0, chunk(j), :] = -c
        beam[1, chunk(j), :] = -s

    def phase_at(layer, r, j):
        return cosr[layer * EXT + r, chunk(j), :], sinr[layer * EXT + r, chunk(j), :]

    def incident(r, _):
        k = (pv[...] * (row * ROWS + r - HALO)) & (NX - 1)
        sa, ca = sincos((k - NX // 2).astype(jnp.float32) * (2.0 * math.pi / NX))
        for j in range(16):
            c, s = phase_at(0, r, j)
            a = sa * s - ca * c
            b = -(sa * c + ca * s)
            er, ei = beam[0, chunk(j), :], beam[1, chunk(j), :]
            u[r, 0, padded(j), :] = er * a - ei * b
            u[r, 1, padded(j), :] = ei * a + er * b
        return 0

    lax.fori_loop(0, EXT, incident, 0)
    fill_pads(u, EXT)
    clear_outside(row, u, HALO, EXT)

    def write_v(r, j, re, im):
        c, s = phase_at(1, r, j)
        v[r, 0, padded(j), :] = re * c - im * s
        v[r, 1, padded(j), :] = re * s + im * c

    step(row, u, EXT, HALO, 8, (l1, l2, l3), rate_scale, write_v)
    fill_pads(v, EXT)
    clear_outside(row, v, HALO, EXT)

    def write_last(r, j, re, im):
        c, s = phase_at(2, r, j)
        w2[r, 0, padded(j), :] = re * c - im * s
        w2[r, 1, padded(j), :] = re * s + im * c

    step(row, v, EXT, HALO, 4, (l1, l2, l3), rate_scale, write_last)
    for r in range(4):
        for k in range(2):
            last_low[r, k] = w2[HALO + r, k, 8:136, :]
            last_high[r, k] = w2[HALO + 4 + r, k, 8:136, :]

    def term(layer, adjoint, stored):
        def body(i, _):
            for r in (2 * i, 2 * i + 1):
                x = adjoint(r, 1) * stored(r, 0) - adjoint(r, 0) * stored(r, 1)
                x = x.T
                x = (x[:TILES] + x[TILES:2 * TILES]) + (x[2 * TILES:3 * TILES] + x[3 * TILES:])
                terms[pl.ds(layer * ROWS + r, TILES, stride=LAYERS * ROWS), :] = x
            return 0

        lax.fori_loop(0, ROWS // 2, body, 0)

    def own(ref):
        return lambda r, k: ref[HALO + r, k, 8:136, :]

    term(2, lambda r, k: w1[HALO + r, k], own(w2))

    def back(r, _):
        for j in range(16):
            c, s = phase_at(2, r, j)
            re, im = w1[r, 0, chunk(j), :], w1[r, 1, chunk(j), :]
            w[r, 0, padded(j), :] = re * c + im * s
            w[r, 1, padded(j), :] = im * c - re * s
        return 0

    lax.fori_loop(0, EXT, back, 0)
    fill_pads(w, EXT)
    clear_outside(row, w, HALO, EXT)

    def mid(r, j, re, im):
        c, s = phase_at(1, r, j)
        raw[r - 4, 0, chunk(j), :] = re
        raw[r - 4, 1, chunk(j), :] = im
        w2[r, 0, padded(j), :] = re * c + im * s
        w2[r, 1, padded(j), :] = im * c - re * s

    step(row, w, EXT, HALO, 8, (l1, l2, l3), -rate_scale, mid)
    fill_pads(w2, EXT)
    clear_outside(row, w2, HALO, EXT)
    term(1, lambda r, k: raw[r + 4, k], own(v))

    def final(r, j, re, im):
        raw[r - 4, 0, chunk(j), :] = re
        raw[r - 4, 1, chunk(j), :] = im

    step(row, w2, EXT, HALO, 4, (l1, l2, l3), -rate_scale, final)
    term(0, lambda r, k: raw[r + 4, k], own(u))


def deal_kernel(mine, out):
    for t in range(TILES):
        x = mine[:, 128 * t:128 * (t + 1)]
        out[t // 2, t % 2] = x
        out[PLANE + t // 2, t % 2] = x


def pick_kernel(order, got, out):
    for layer in range(LAYERS):
        for t in range(2):
            x = got[order[layer], t]
            for d in range(PLANE):
                out[d, t, layer] = x


def gather_kernel(order, parts, out):
    out[...] = jnp.zeros_like(out)
    for layer in range(LAYERS):
        for t in range(2):
            x = [parts[d, t, layer] for d in range(PLANE)]
            while len(x) > 1:
                x = [a + b for a, b in zip(x[::2], x[1::2])]
            out[order[layer], t] = x[0]


def finish_kernel(got, out):
    for t in range(TILES):
        out[:, 128 * t:128 * (t + 1)] = got[t // 2, t % 2] + got[PLANE + t // 2, t % 2]


def vm():
    return pl.BlockSpec(memory_space=pltpu.VMEM)


def sm():
    return pl.BlockSpec(memory_space=pltpu.SMEM)


def shape(*dims):
    return jax.ShapeDtypeStruct(dims, jnp.float32)


def field(rows):
    return shape(rows, 2, 128, 128)


def scr(*dims):
    return pltpu.VMEM(dims, jnp.float32)


def wide(rows):
    return scr(rows, 2, PAD, 128)


def call(kernel, ins, outs, scratch, mib):
    return pl.pallas_call(
        kernel, out_shape=outs, in_specs=ins, out_specs=jax.tree.map(lambda _: vm(), outs),
        scratch_shapes=scratch,
        compiler_params=pltpu.CompilerParams(vmem_limit_bytes=mib << 20),
        cost_estimate=pl.CostEstimate(flops=20_000_000, bytes_accessed=4 << 20, transcendentals=0),
    )


def forward_and_back(angles, depth_order, slices, cotangent):
    row = lax.axis_index("row").astype(jnp.int32).reshape(1)
    n_row = lax.axis_size("row")
    groups = [list(range(g * PLANE, (g + 1) * PLANE)) for g in range(2)]

    def to_next(x, by):
        return lax.ppermute(x, "row", [(i, i + by) for i in range(n_row - by)])

    def to_prev(x, by):
        return lax.ppermute(x, "row", [(i + by, i) for i in range(n_row - by)])

    def exchange(x, groups=None):
        flat = x.reshape(-1, 128)
        flat = lax.all_to_all(flat, "illum", 0, 0, axis_index_groups=groups, tiled=True)
        return flat.reshape(x.shape)

    dealt = call(deal_kernel, [vm()], shape(2 * PLANE, 2, ROWS, 128), [], 4)(slices[0])
    got = exchange(dealt)
    cot = cotangent.reshape(8, ROWS, TILES, 128).transpose(0, 2, 1, 3).reshape(-1, 128)
    own, low, high = call(
        split_kernel, [vm()], (field(8), field(4), field(4)), [], 6)(cot)
    top, bot = to_next(own, 1), to_prev(own, 1)
    top2, bot2 = to_next(high, 2), to_prev(low, 2)
    piece = call(pick_kernel, [sm(), vm()], shape(PLANE, 2, LAYERS, ROWS, 128), [],
                 4)(depth_order, got)
    phases = exchange(piece, groups).reshape(-1, 128)
    ph_top, ph_bot = to_next(phases, 1), to_prev(phases, 1)

    table = scr(TILES * LAYERS * ROWS, 128)
    cos_own, sin_own = call(
        phase_kernel, [vm()], (shape(LAYERS * ROWS, 128, 128),) * 2, [table] * 2,
        5)(phases)
    w1 = call(adjoint_kernel, [sm()] + [vm()] * 5, field(EXT), [wide(32)] * 4,
              20)(row, own, top, bot, top2, bot2)

    pv = jnp.broadcast_to(jnp.repeat(angles[:, 0], TILES)[None], (8, 128))
    qv = jnp.broadcast_to(jnp.repeat(angles[:, 1], TILES)[None], (8, 128))
    spreads = scr(LAYERS * EXT, 128, 128)
    terms, last_low, last_high = call(
        main_kernel, [sm()] + [vm()] * 7,
        (shape(TILES * LAYERS * ROWS, 128), field(4), field(4)),
        [table, table, spreads, spreads, scr(2, 128, 128)] + [wide(EXT)] * 4
        + [scr(16, 2, 128, 128)] + [wide(EXT)] * 3, 40)(
            row, pv, qv, ph_top, ph_bot, cos_own, sin_own, w1)
    r_top, r_bot = to_next(last_high, 1), to_prev(last_low, 1)
    parts = exchange(terms, groups).reshape(PLANE, 2, LAYERS, ROWS, 128)
    send = call(gather_kernel, [sm(), vm()], shape(2 * PLANE, 2, ROWS, 128), [],
                4)(depth_order, parts)
    back = exchange(send)
    out = call(exit_kernel, [sm()] + [vm()] * 4, shape(2048, 128),
               [wide(16)] * 4 + [scr(8, 2, 128, 128)], 12)(
                   row, last_low, last_high, r_top, r_bot)
    grad = call(finish_kernel, [vm()], shape(ROWS, COLS), [], 4)(back)
    out = out.reshape(8, TILES, ROWS, 128).transpose(0, 2, 1, 3)
    return out.reshape(cotangent.shape), grad[None]


def solution(mesh):
    placed = (P("illum", None), P(), P("illum", "row", None), P("illum", None, "row", None))
    return jax.shard_map(
        forward_and_back,
        mesh=mesh,
        in_specs=placed,
        out_specs=(P("illum", None, "row", None), P("illum", "row", None)),
        check_vma=False,
    )
```

```python
import math

import jax
import jax.numpy as jnp
from jax import lax
from jax.experimental import pallas as pl
from jax.experimental.pallas import tpu as pltpu
from jax.sharding import PartitionSpec as P


rate_scale = 0.3
ROWS = 8
COLS = 4096
TILES = COLS // 128
LAYERS = 3
HALO = 8
EXT = ROWS + 2 * HALO
N_ROW = 8
NX = ROWS * N_ROW
PAD = 144
PLANE = 16

SIN_C = (0.9999999996397458, -0.16666666036106006, 0.00833331543673961,
         -0.00019839409893936808, 2.7469726872825416e-06, -2.3138942785856126e-08)
COS_C = (0.9999999953627682, -0.49999991881071015, 0.04166643614419552,
         -0.001388649171259302, 2.4688583708756773e-05, -2.5084304017242627e-07)


def horner(coefs, z):
    r = z * coefs[-1] + coefs[-2]
    for c in coefs[-3::-1]:
        r = r * z + c
    return r


def sincos(x):
    y = x * 0.5
    z = y * y
    s = y * horner(SIN_C, z)
    c = horner(COS_C, z)
    s2 = s + s
    return s2 * c, 1.0 - s2 * s


def chunk(j):
    return slice(8 * j, 8 * j + 8)


def padded(j, shift=0):
    return slice(8 + 8 * j + shift, 16 + 8 * j + shift)


def fill_pads(ref, rows):
    flat = ref.reshape(rows * 2 * PAD, 128)
    tile = lax.broadcasted_iota(jnp.int32, (rows * 2, 128), 1) & (TILES - 1)
    high = flat[pl.ds(135, rows * 2, stride=PAD), :]
    low = flat[pl.ds(8, rows * 2, stride=PAD), :]
    flat[pl.ds(7, rows * 2, stride=PAD), :] = jnp.where(tile == 0, 0.0, pltpu.roll(high, 1, 1))
    flat[pl.ds(136, rows * 2, stride=PAD), :] = jnp.where(
        tile == TILES - 1, 0.0, pltpu.roll(low, 127, 1))


def clear_outside(row, ref, base, rows):
    for at in (base - 1 - ROWS * row, base + NX - ROWS * row):
        @pl.when((at >= 0) & (at < rows))
        def _(at=at):
            ref[at] = jnp.zeros((2, PAD, 128), jnp.float32)


def lap_pair(src, r, k, j):
    v = [src[r + q, k, padded(j), :] for q in (-1, 0, 1, 2)]
    out = []
    for q in (0, 1):
        side = src[r + q, k, padded(j, -1), :] + src[r + q, k, padded(j, 1), :]
        out.append((v[q] + v[q + 2]) + side - 4.0 * v[q + 1])
    return out


def step(row, src, rows, base, h, powers, factor, write):
    prev = src
    for n, dst in enumerate(powers):
        lo, count = base - h + 1 + n, ROWS + 2 * (h - 1 - n)

        def body(i, _, prev=prev, dst=dst, lo=lo):
            r = lo + 2 * i
            for k in range(2):
                for j in range(16):
                    a, b = lap_pair(prev, r, k, j)
                    dst[r, k, padded(j), :] = a
                    dst[r + 1, k, padded(j), :] = b
            return 0

        lax.fori_loop(0, count // 2, body, 0)
        fill_pads(dst, rows)
        clear_outside(row, dst, base, rows)
        prev = dst
    l1, l2, l3 = powers
    c1, c2, c3, c4 = factor, -factor**2 / 2, -factor**3 / 6, factor**4 / 24
    lo = base - h + 4

    def last(i, _):
        r = lo + 2 * i
        for j in range(16):
            l4 = [lap_pair(l3, r, k, j) for k in range(2)]
            for q in (0, 1):
                even, odd = [], []
                for k in range(2):
                    at = (r + q, k, padded(j), slice(None))
                    even.append(src[at] + (c2 * l2[at] + c4 * l4[k][q]))
                    odd.append(c1 * l1[at] + c3 * l3[at])
                write(r + q, j, even[0] - odd[1], even[1] + odd[0])
        return 0

    lax.fori_loop(0, (ROWS + 2 * (h - 4)) // 2, last, 0)


def natural(g, k, r):
    return pl.ds((g * 2 + k) * TILES * ROWS + r, TILES, stride=ROWS)


def turn_rows(cot, out):
    def body(r, _):
        for k in range(2):
            out[r, k] = jnp.concatenate([cot[natural(g, k, r), :] for g in range(4)], axis=0).T
        return 0

    lax.fori_loop(0, ROWS, body, 0)


def split_kernel(ids, cot, out, send_e, send_o):
    turn_rows(cot, out)
    upper = (ids[0] >> 1) & 1
    for r in range(4):
        send_e[r] = out[r + 4 * (1 - upper)]
        send_o[r] = out[r + 4 * upper]


def halo_kernel(cot_e, cot_o, out_e, out_o):
    turn_rows(cot_e, out_e)
    turn_rows(cot_o, out_o)


def put(dst, at, src, n):
    def body(r, _):
        for k in range(2):
            dst[at + r, k, 8:136, :] = src[r, k]
        return 0

    lax.fori_loop(0, n, body, 0)


def adjoint_kernel(ids, own, halo_e, halo_o, far_e, far_o, out, u, l1, l2, l3):
    row = ids[0]
    odd, upper = row & 1, (row >> 1) & 1
    put(u, 12, own, 8)
    put(u, 20 - 16 * odd, halo_e, 8)
    put(u, 4 + 16 * odd, halo_o, 8)
    put(u, 28 - 28 * upper, far_e, 4)
    put(u, 28 * upper, far_o, 4)
    fill_pads(u, 32)

    def write(r, j, re, im):
        out[r - 4, 0, chunk(j), :] = re
        out[r - 4, 1, chunk(j), :] = im

    step(row, u, 32, 12, 12, (l1, l2, l3), -rate_scale, write)


def exit_kernel(ids, sent_e, sent_o, got_e, got_o, out, u, l1, l2, l3, res):
    row = ids[0]
    odd = row & 1
    put(u, 8 - 4 * odd, sent_e, 4)
    put(u, 4 + 4 * odd, sent_o, 4)
    put(u, 12 - 12 * odd, got_e, 4)
    put(u, 12 * odd, got_o, 4)
    fill_pads(u, 16)

    def write(r, j, re, im):
        res[r - 4, 0, chunk(j), :] = re
        res[r - 4, 1, chunk(j), :] = im

    step(row, u, 16, 4, 4, (l1, l2, l3), rate_scale, write)

    def body(r, _):
        for k in range(2):
            x = res[r, k].T
            for g in range(4):
                out[natural(g, k, r), :] = x[g * TILES:(g + 1) * TILES]
        return 0

    lax.fori_loop(0, ROWS, body, 0)


def trig_tables(phases, cos_n, sin_n):
    def body(i, _):
        at = pl.ds(pl.multiple_of(i * 24, 8), 24)
        s, c = sincos(phases[at, :])
        sin_n[at, :] = s
        cos_n[at, :] = c
        return 0

    lax.fori_loop(0, TILES, body, 0)


def spread(ref, n):
    x = ref[pl.ds(n, TILES, stride=LAYERS * ROWS), :]
    return jnp.concatenate([x] * 4, axis=0).T


def phase_kernel(phases, cos_out, sin_out, cos_n, sin_n):
    trig_tables(phases, cos_n, sin_n)

    def body(i, _):
        for n in (2 * i, 2 * i + 1):
            cos_out[n] = spread(cos_n, n)
            sin_out[n] = spread(sin_n, n)
        return 0

    lax.fori_loop(0, LAYERS * ROWS // 2, body, 0)


def main_kernel(ids, pv, qv, ph_e, ph_o, cos_own, sin_own, w1,
                terms, last_e, last_o,
                cos_n, sin_n, cosr, sinr, beam, u, v, w, w2, raw, l1, l2, l3):
    row = ids[0]
    odd = row & 1
    for ph, above in ((ph_e, odd), (ph_o, 1 - odd)):
        trig_tables(ph, cos_n, sin_n)
        first = (HALO + ROWS) * (1 - above)
        for layer in range(LAYERS):
            lo, count = (4 * above, 4) if layer == 1 else (0, 8)

            def body(i, _, layer=layer, first=first, lo=lo):
                for q in range(2):
                    r = lo + 2 * i + q
                    cosr[layer * EXT + first + r] = spread(cos_n, layer * ROWS + r)
                    sinr[layer * EXT + first + r] = spread(sin_n, layer * ROWS + r)
                return 0

            lax.fori_loop(0, count // 2, body, 0)
    for layer in range(LAYERS):
        def copy(r, _, layer=layer):
            cosr[layer * EXT + HALO + r] = cos_own[layer * ROWS + r]
            sinr[layer * EXT + HALO + r] = sin_own[layer * ROWS + r]
            return 0

        lax.fori_loop(0, ROWS, copy, 0)

    lane = lax.broadcasted_iota(jnp.int32, (8, 128), 1)
    sub = lax.broadcasted_iota(jnp.int32, (8, 128), 0)
    for j in range(16):
        col = (lane & (TILES - 1)) * 128 + sub + 8 * j
        k = (qv[...] * col) & (COLS - 1)
        s, c = sincos((k - COLS // 2).astype(jnp.float32) * (2.0 * math.pi / COLS))
        beam[0, chunk(j), :] = -c
        beam[1, chunk(j), :] = -s

    def phase_at(layer, r, j):
        return cosr[layer * EXT + r, chunk(j), :], sinr[layer * EXT + r, chunk(j), :]

    def incident(r, _):
        k = (pv[...] * (row * ROWS + r - HALO)) & (NX - 1)
        sa, ca = sincos((k - NX // 2).astype(jnp.float32) * (2.0 * math.pi / NX))
        for j in range(16):
            c, s = phase_at(0, r, j)
            a = sa * s - ca * c
            b = -(sa * c + ca * s)
            er, ei = beam[0, chunk(j), :], beam[1, chunk(j), :]
            u[r, 0, padded(j), :] = er * a - ei * b
            u[r, 1, padded(j), :] = ei * a + er * b
        return 0

    lax.fori_loop(0, EXT, incident, 0)
    fill_pads(u, EXT)
    clear_outside(row, u, HALO, EXT)

    def write_v(r, j, re, im):
        c, s = phase_at(1, r, j)
        v[r, 0, padded(j), :] = re * c - im * s
        v[r, 1, padded(j), :] = re * s + im * c

    step(row, u, EXT, HALO, 8, (l1, l2, l3), rate_scale, write_v)
    fill_pads(v, EXT)
    clear_outside(row, v, HALO, EXT)

    def write_last(r, j, re, im):
        c, s = phase_at(2, r, j)
        w2[r, 0, padded(j), :] = re * c - im * s
        w2[r, 1, padded(j), :] = re * s + im * c

    step(row, v, EXT, HALO, 4, (l1, l2, l3), rate_scale, write_last)
    for r in range(4):
        for k in range(2):
            last_e[r, k] = w2[HALO + r + 4 * (1 - odd), k, 8:136, :]
            last_o[r, k] = w2[HALO + r + 4 * odd, k, 8:136, :]

    def term(layer, adjoint, stored):
        def body(i, _):
            for r in (2 * i, 2 * i + 1):
                x = adjoint(r, 1) * stored(r, 0) - adjoint(r, 0) * stored(r, 1)
                x = x.T
                x = (x[:TILES] + x[TILES:2 * TILES]) + (x[2 * TILES:3 * TILES] + x[3 * TILES:])
                terms[pl.ds(layer * ROWS + r, TILES, stride=LAYERS * ROWS), :] = x
            return 0

        lax.fori_loop(0, ROWS // 2, body, 0)

    def own(ref):
        return lambda r, k: ref[HALO + r, k, 8:136, :]

    term(2, lambda r, k: w1[HALO + r, k], own(w2))

    def back(r, _):
        for j in range(16):
            c, s = phase_at(2, r, j)
            re, im = w1[r, 0, chunk(j), :], w1[r, 1, chunk(j), :]
            w[r, 0, padded(j), :] = re * c + im * s
            w[r, 1, padded(j), :] = im * c - re * s
        return 0

    lax.fori_loop(0, EXT, back, 0)
    fill_pads(w, EXT)
    clear_outside(row, w, HALO, EXT)

    def mid(r, j, re, im):
        c, s = phase_at(1, r, j)
        raw[r - 4, 0, chunk(j), :] = re
        raw[r - 4, 1, chunk(j), :] = im
        w2[r, 0, padded(j), :] = re * c + im * s
        w2[r, 1, padded(j), :] = im * c - re * s

    step(row, w, EXT, HALO, 8, (l1, l2, l3), -rate_scale, mid)
    fill_pads(w2, EXT)
    clear_outside(row, w2, HALO, EXT)
    term(1, lambda r, k: raw[r + 4, k], own(v))

    def final(r, j, re, im):
        raw[r - 4, 0, chunk(j), :] = re
        raw[r - 4, 1, chunk(j), :] = im

    step(row, w2, EXT, HALO, 4, (l1, l2, l3), -rate_scale, final)
    term(0, lambda r, k: raw[r + 4, k], own(u))


def deal_kernel(mine, out):
    for t in range(TILES):
        out[t // 2, t % 2] = mine[:, 128 * t:128 * (t + 1)]


def pick_kernel(ids, order, got, out):
    for layer in range(LAYERS):
        held = (order[layer] >> 4) == ids[1]
        for t in range(2):
            x = got[order[layer] & (PLANE - 1), t]
            out[t, layer] = jnp.where(held, x, jnp.zeros_like(x))


def copies_kernel(mine, other, out):
    x = mine[...] + other[...]
    for d in range(PLANE):
        out[d] = x


def sum_kernel(parts, out):
    for layer in range(LAYERS):
        for t in range(2):
            x = [parts[d, t, layer] for d in range(PLANE)]
            while len(x) > 1:
                x = [a + b for a, b in zip(x[::2], x[1::2])]
            out[t, layer] = x[0]


def address_kernel(ids, order, mine, other, out):
    out[...] = jnp.zeros_like(out)
    for layer in range(LAYERS):
        @pl.when((order[layer] >> 4) == ids[1])
        def _(layer=layer):
            for t in range(2):
                out[order[layer] & (PLANE - 1), t] = mine[t, layer] + other[t, layer]


def finish_kernel(got, out):
    for t in range(TILES):
        out[:, 128 * t:128 * (t + 1)] = got[t // 2, t % 2]


def vm():
    return pl.BlockSpec(memory_space=pltpu.VMEM)


def sm():
    return pl.BlockSpec(memory_space=pltpu.SMEM)


def shape(*dims):
    return jax.ShapeDtypeStruct(dims, jnp.float32)


def field(rows):
    return shape(rows, 2, 128, 128)


def scr(*dims):
    return pltpu.VMEM(dims, jnp.float32)


def wide(rows):
    return scr(rows, 2, PAD, 128)


def call(kernel, ins, outs, scratch, mib):
    return pl.pallas_call(
        kernel, out_shape=outs, in_specs=ins, out_specs=jax.tree.map(lambda _: vm(), outs),
        scratch_shapes=scratch,
        compiler_params=pltpu.CompilerParams(vmem_limit_bytes=mib << 20),
        cost_estimate=pl.CostEstimate(flops=20_000_000, bytes_accessed=4 << 20, transcendentals=0),
    )


def forward_and_back(angles, depth_order, slices, cotangent):
    n_row = lax.axis_size("row")
    group = lax.axis_index("illum") // PLANE
    ids = jnp.stack([lax.axis_index("row"), group]).astype(jnp.int32)
    groups = [list(range(g * PLANE, (g + 1) * PLANE)) for g in range(2)]
    swap = [(i, (i + PLANE) % (2 * PLANE)) for i in range(2 * PLANE)]

    def meet(x_e, x_o, by):
        even = [(i, i ^ by) for i in range(n_row)]
        odd = [(i, i + by) for i in range(by, n_row - by) if i & by]
        odd = odd + [(j, i) for i, j in odd]
        got_o = lax.ppermute(x_o, "row", odd)
        got_e = lax.ppermute(x_e, "row", even)
        return got_e, got_o

    def exchange(x):
        flat = x.reshape(-1, 128)
        flat = lax.all_to_all(flat, "illum", 0, 0, axis_index_groups=groups, tiled=True)
        return flat.reshape(x.shape)

    def rows_first(x):
        return x.reshape(8, ROWS, TILES, 128).transpose(0, 2, 1, 3).reshape(-1, 128)

    cot_e, cot_o = meet(cotangent, cotangent, 1)
    dealt = call(deal_kernel, [vm()], shape(PLANE, 2, ROWS, 128), [], 4)(slices[0])
    got = exchange(dealt)
    own, send_e, send_o = call(
        split_kernel, [sm(), vm()], (field(8), field(4), field(4)), [], 6)(
            ids, rows_first(cotangent))
    piece = call(pick_kernel, [sm(), sm(), vm()], shape(2, LAYERS, ROWS, 128), [],
                 2)(ids, depth_order, got)
    piece_z = lax.ppermute(piece, "illum", swap)
    far_e, far_o = meet(send_e, send_o, 2)
    halo_e, halo_o = call(halo_kernel, [vm()] * 2, (field(8),) * 2, [], 6)(
        rows_first(cot_e), rows_first(cot_o))
    whole = call(copies_kernel, [vm()] * 2, shape(PLANE, 2, LAYERS, ROWS, 128), [],
                 2)(piece, piece_z)
    phases = exchange(whole).reshape(-1, 128)
    ph_e, ph_o = meet(phases, phases, 1)

    table = scr(TILES * LAYERS * ROWS, 128)
    cos_own, sin_own = call(
        phase_kernel, [vm()], (shape(LAYERS * ROWS, 128, 128),) * 2, [table] * 2,
        5)(phases)
    w1 = call(adjoint_kernel, [sm()] + [vm()] * 5, field(EXT), [wide(32)] * 4,
              20)(ids, own, halo_e, halo_o, far_e, far_o)

    pv = jnp.broadcast_to(jnp.repeat(angles[:, 0], TILES)[None], (8, 128))
    qv = jnp.broadcast_to(jnp.repeat(angles[:, 1], TILES)[None], (8, 128))
    spreads = scr(LAYERS * EXT, 128, 128)
    terms, last_e, last_o = call(
        main_kernel, [sm()] + [vm()] * 7,
        (shape(TILES * LAYERS * ROWS, 128), field(4), field(4)),
        [table, table, spreads, spreads, scr(2, 128, 128)] + [wide(EXT)] * 4
        + [scr(16, 2, 128, 128)] + [wide(EXT)] * 3, 40)(
            ids, pv, qv, ph_e, ph_o, cos_own, sin_own, w1)
    parts = exchange(terms).reshape(PLANE, 2, LAYERS, ROWS, 128)
    half = call(sum_kernel, [vm()], shape(2, LAYERS, ROWS, 128), [], 2)(parts)
    half_z = lax.ppermute(half, "illum", swap)
    r_e, r_o = meet(last_e, last_o, 1)
    send = call(address_kernel, [sm(), sm()] + [vm()] * 2, shape(PLANE, 2, ROWS, 128), [],
                2)(ids, depth_order, half, half_z)
    back = exchange(send)
    out = call(exit_kernel, [sm()] + [vm()] * 4, shape(2048, 128),
               [wide(16)] * 4 + [scr(8, 2, 128, 128)], 12)(
                   ids, last_e, last_o, r_e, r_o)
    grad = call(finish_kernel, [vm()], shape(ROWS, COLS), [], 2)(back)
    out = out.reshape(8, TILES, ROWS, 128).transpose(0, 2, 1, 3)
    return out.reshape(cotangent.shape), grad[None]


def solution(mesh):
    placed = (P("illum", None), P(), P("illum", "row", None), P("illum", None, "row", None))
    return jax.shard_map(
        forward_and_back,
        mesh=mesh,
        in_specs=placed,
        out_specs=(P("illum", None, "row", None), P("illum", "row", None)),
        check_vma=False,
    )
```

```python
import math

import jax
import jax.numpy as jnp
from jax import lax
from jax.experimental import pallas as pl
from jax.experimental.pallas import tpu as pltpu
from jax.sharding import PartitionSpec as P


rate_scale = 0.3
ROWS = 8
COLS = 4096
TILES = COLS // 128
LAYERS = 3
HALO = 8
EXT = ROWS + 2 * HALO
N_ROW = 8
NX = ROWS * N_ROW
PAD = 144
PLANE = 16

SIN_C = (0.9999999996397458, -0.16666666036106006, 0.00833331543673961,
         -0.00019839409893936808, 2.7469726872825416e-06, -2.3138942785856126e-08)
COS_C = (0.9999999953627682, -0.49999991881071015, 0.04166643614419552,
         -0.001388649171259302, 2.4688583708756773e-05, -2.5084304017242627e-07)


def horner(coefs, z):
    r = z * coefs[-1] + coefs[-2]
    for c in coefs[-3::-1]:
        r = r * z + c
    return r


def sincos(x):
    y = x * 0.5
    z = y * y
    s = y * horner(SIN_C, z)
    c = horner(COS_C, z)
    s2 = s + s
    return s2 * c, 1.0 - s2 * s


def chunk(j):
    return slice(8 * j, 8 * j + 8)


def padded(j, shift=0):
    return slice(8 + 8 * j + shift, 16 + 8 * j + shift)


def fill_pads(ref, rows):
    flat = ref.reshape(rows * 2 * PAD, 128)
    tile = lax.broadcasted_iota(jnp.int32, (rows * 2, 128), 1) & (TILES - 1)
    high = flat[pl.ds(135, rows * 2, stride=PAD), :]
    low = flat[pl.ds(8, rows * 2, stride=PAD), :]
    flat[pl.ds(7, rows * 2, stride=PAD), :] = jnp.where(tile == 0, 0.0, pltpu.roll(high, 1, 1))
    flat[pl.ds(136, rows * 2, stride=PAD), :] = jnp.where(
        tile == TILES - 1, 0.0, pltpu.roll(low, 127, 1))


def clear_outside(row, ref, base, rows):
    for at in (base - 1 - ROWS * row, base + NX - ROWS * row):
        @pl.when((at >= 0) & (at < rows))
        def _(at=at):
            ref[at] = jnp.zeros((2, PAD, 128), jnp.float32)


def lap_pair(src, r, k, j):
    v = [src[r + q, k, padded(j), :] for q in (-1, 0, 1, 2)]
    out = []
    for q in (0, 1):
        side = src[r + q, k, padded(j, -1), :] + src[r + q, k, padded(j, 1), :]
        out.append((v[q] + v[q + 2]) + side - 4.0 * v[q + 1])
    return out


def step(row, src, rows, base, h, powers, factor, write):
    prev = src
    for n, dst in enumerate(powers):
        lo, count = base - h + 1 + n, ROWS + 2 * (h - 1 - n)

        def body(i, _, prev=prev, dst=dst, lo=lo):
            r = lo + 2 * i
            for k in range(2):
                for j in range(16):
                    a, b = lap_pair(prev, r, k, j)
                    dst[r, k, padded(j), :] = a
                    dst[r + 1, k, padded(j), :] = b
            return 0

        lax.fori_loop(0, count // 2, body, 0)
        fill_pads(dst, rows)
        clear_outside(row, dst, base, rows)
        prev = dst
    l1, l2, l3 = powers
    c1, c2, c3, c4 = factor, -factor**2 / 2, -factor**3 / 6, factor**4 / 24
    lo = base - h + 4

    def last(i, _):
        r = lo + 2 * i
        for j in range(16):
            l4 = [lap_pair(l3, r, k, j) for k in range(2)]
            for q in (0, 1):
                even, odd = [], []
                for k in range(2):
                    at = (r + q, k, padded(j), slice(None))
                    even.append(src[at] + (c2 * l2[at] + c4 * l4[k][q]))
                    odd.append(c1 * l1[at] + c3 * l3[at])
                write(r + q, j, even[0] - odd[1], even[1] + odd[0])
        return 0

    lax.fori_loop(0, (ROWS + 2 * (h - 4)) // 2, last, 0)


def natural(g, k, r):
    return pl.ds((g * 2 + k) * TILES * ROWS + r, TILES, stride=ROWS)


def turn_rows(cot, out):
    def body(r, _):
        for k in range(2):
            out[r, k] = jnp.concatenate([cot[natural(g, k, r), :] for g in range(4)], axis=0).T
        return 0

    lax.fori_loop(0, ROWS, body, 0)


def split_kernel(ids, cot, out, send_e, send_o):
    turn_rows(cot, out)
    upper = (ids[0] >> 1) & 1
    for r in range(4):
        send_e[r] = out[r + 4 * (1 - upper)]
        send_o[r] = out[r + 4 * upper]


def halo_kernel(cot_e, cot_o, out_e, out_o):
    turn_rows(cot_e, out_e)
    turn_rows(cot_o, out_o)


def put(dst, at, src, n):
    def body(r, _):
        for k in range(2):
            dst[at + r, k, 8:136, :] = src[r, k]
        return 0

    lax.fori_loop(0, n, body, 0)


def adjoint_kernel(ids, own, halo_e, halo_o, far_e, far_o, out, u, l1, l2, l3):
    row = ids[0]
    odd, upper = row & 1, (row >> 1) & 1
    put(u, 12, own, 8)
    put(u, 20 - 16 * odd, halo_e, 8)
    put(u, 4 + 16 * odd, halo_o, 8)
    put(u, 28 - 28 * upper, far_e, 4)
    put(u, 28 * upper, far_o, 4)
    fill_pads(u, 32)

    def write(r, j, re, im):
        out[r - 4, 0, chunk(j), :] = re
        out[r - 4, 1, chunk(j), :] = im

    step(row, u, 32, 12, 12, (l1, l2, l3), -rate_scale, write)


def exit_kernel(ids, sent_e, sent_o, got_e, got_o, out, u, l1, l2, l3, res):
    row = ids[0]
    odd = row & 1
    put(u, 8 - 4 * odd, sent_e, 4)
    put(u, 4 + 4 * odd, sent_o, 4)
    put(u, 12 - 12 * odd, got_e, 4)
    put(u, 12 * odd, got_o, 4)
    fill_pads(u, 16)

    def write(r, j, re, im):
        res[r - 4, 0, chunk(j), :] = re
        res[r - 4, 1, chunk(j), :] = im

    step(row, u, 16, 4, 4, (l1, l2, l3), rate_scale, write)

    def body(r, _):
        for k in range(2):
            x = res[r, k].T
            for g in range(4):
                out[natural(g, k, r), :] = x[g * TILES:(g + 1) * TILES]
        return 0

    lax.fori_loop(0, ROWS, body, 0)


def trig_tables(phases, cos_n, sin_n):
    def body(i, _):
        at = pl.ds(pl.multiple_of(i * 24, 8), 24)
        s, c = sincos(phases[at, :])
        sin_n[at, :] = s
        cos_n[at, :] = c
        return 0

    lax.fori_loop(0, TILES, body, 0)


def spread(ref, n):
    x = ref[pl.ds(n, TILES, stride=LAYERS * ROWS), :]
    return jnp.concatenate([x] * 4, axis=0).T


def phase_kernel(phases, cos_out, sin_out, cos_n, sin_n):
    trig_tables(phases, cos_n, sin_n)

    def body(i, _):
        for n in (2 * i, 2 * i + 1):
            cos_out[n] = spread(cos_n, n)
            sin_out[n] = spread(sin_n, n)
        return 0

    lax.fori_loop(0, LAYERS * ROWS // 2, body, 0)


def main_kernel(ids, angles, ph_e, ph_o, cos_own, sin_own, w1,
                terms, last_e, last_o,
                cos_n, sin_n, cosr, sinr, beam, u, v, w, w2, raw, l1, l2, l3):
    row = ids[0]
    odd = row & 1
    for ph, above in ((ph_e, odd), (ph_o, 1 - odd)):
        trig_tables(ph, cos_n, sin_n)
        first = (HALO + ROWS) * (1 - above)
        for layer in range(LAYERS):
            lo, count = (4 * above, 4) if layer == 1 else (0, 8)

            def body(i, _, layer=layer, first=first, lo=lo):
                for q in range(2):
                    r = lo + 2 * i + q
                    cosr[layer * EXT + first + r] = spread(cos_n, layer * ROWS + r)
                    sinr[layer * EXT + first + r] = spread(sin_n, layer * ROWS + r)
                return 0

            lax.fori_loop(0, count // 2, body, 0)
    for layer in range(LAYERS):
        def copy(r, _, layer=layer):
            cosr[layer * EXT + HALO + r] = cos_own[layer * ROWS + r]
            sinr[layer * EXT + HALO + r] = sin_own[layer * ROWS + r]
            return 0

        lax.fori_loop(0, ROWS, copy, 0)

    lane = lax.broadcasted_iota(jnp.int32, (8, 128), 1)
    sub = lax.broadcasted_iota(jnp.int32, (8, 128), 0)
    beam_of = lane >> 5
    pv, qv = [
        jnp.where(beam_of < 2,
                  jnp.where(beam_of == 0, angles[0, n], angles[1, n]),
                  jnp.where(beam_of == 2, angles[2, n], angles[3, n]))
        for n in range(2)
    ]
    for j in range(16):
        col = (lane & (TILES - 1)) * 128 + sub + 8 * j
        k = (qv * col) & (COLS - 1)
        s, c = sincos((k - COLS // 2).astype(jnp.float32) * (2.0 * math.pi / COLS))
        beam[0, chunk(j), :] = -c
        beam[1, chunk(j), :] = -s

    def phase_at(layer, r, j):
        return cosr[layer * EXT + r, chunk(j), :], sinr[layer * EXT + r, chunk(j), :]

    def incident(r, _):
        k = (pv * (row * ROWS + r - HALO)) & (NX - 1)
        sa, ca = sincos((k - NX // 2).astype(jnp.float32) * (2.0 * math.pi / NX))
        for j in range(16):
            c, s = phase_at(0, r, j)
            a = sa * s - ca * c
            b = -(sa * c + ca * s)
            er, ei = beam[0, chunk(j), :], beam[1, chunk(j), :]
            u[r, 0, padded(j), :] = er * a - ei * b
            u[r, 1, padded(j), :] = ei * a + er * b
        return 0

    lax.fori_loop(0, EXT, incident, 0)
    fill_pads(u, EXT)
    clear_outside(row, u, HALO, EXT)

    def write_v(r, j, re, im):
        c, s = phase_at(1, r, j)
        v[r, 0, padded(j), :] = re * c - im * s
        v[r, 1, padded(j), :] = re * s + im * c

    step(row, u, EXT, HALO, 8, (l1, l2, l3), rate_scale, write_v)
    fill_pads(v, EXT)
    clear_outside(row, v, HALO, EXT)

    def write_last(r, j, re, im):
        c, s = phase_at(2, r, j)
        w2[r, 0, padded(j), :] = re * c - im * s
        w2[r, 1, padded(j), :] = re * s + im * c

    step(row, v, EXT, HALO, 4, (l1, l2, l3), rate_scale, write_last)
    for r in range(4):
        for k in range(2):
            last_e[r, k] = w2[HALO + r + 4 * (1 - odd), k, 8:136, :]
            last_o[r, k] = w2[HALO + r + 4 * odd, k, 8:136, :]

    def term(layer, adjoint, stored):
        def body(i, _):
            for r in (2 * i, 2 * i + 1):
                x = adjoint(r, 1) * stored(r, 0) - adjoint(r, 0) * stored(r, 1)
                x = x.T
                x = (x[:TILES] + x[TILES:2 * TILES]) + (x[2 * TILES:3 * TILES] + x[3 * TILES:])
                terms[pl.ds(layer * ROWS + r, TILES, stride=LAYERS * ROWS), :] = x
            return 0

        lax.fori_loop(0, ROWS // 2, body, 0)

    def own(ref):
        return lambda r, k: ref[HALO + r, k, 8:136, :]

    term(2, lambda r, k: w1[HALO + r, k], own(w2))

    def back(r, _):
        for j in range(16):
            c, s = phase_at(2, r, j)
            re, im = w1[r, 0, chunk(j), :], w1[r, 1, chunk(j), :]
            w[r, 0, padded(j), :] = re * c + im * s
            w[r, 1, padded(j), :] = im * c - re * s
        return 0

    lax.fori_loop(0, EXT, back, 0)
    fill_pads(w, EXT)
    clear_outside(row, w, HALO, EXT)

    def mid(r, j, re, im):
        c, s = phase_at(1, r, j)
        raw[r - 4, 0, chunk(j), :] = re
        raw[r - 4, 1, chunk(j), :] = im
        w2[r, 0, padded(j), :] = re * c + im * s
        w2[r, 1, padded(j), :] = im * c - re * s

    step(row, w, EXT, HALO, 8, (l1, l2, l3), -rate_scale, mid)
    fill_pads(w2, EXT)
    clear_outside(row, w2, HALO, EXT)
    term(1, lambda r, k: raw[r + 4, k], own(v))

    def final(r, j, re, im):
        raw[r - 4, 0, chunk(j), :] = re
        raw[r - 4, 1, chunk(j), :] = im

    step(row, w2, EXT, HALO, 4, (l1, l2, l3), -rate_scale, final)
    term(0, lambda r, k: raw[r + 4, k], own(u))


def deal_kernel(mine, other, out):
    for t in range(TILES):
        out[t // 2, 0, t % 2] = mine[t]
        out[t // 2, 1, t % 2] = other[t]


def pick_kernel(ids, order, got, out):
    for layer in range(LAYERS):
        for t in range(2):
            x = got[order[layer] & (PLANE - 1), (order[layer] >> 4) ^ ids[1], t]
            for d in range(PLANE):
                out[d, t, layer] = x


def sum_kernel(parts, out):
    for layer in range(LAYERS):
        for t in range(2):
            x = [parts[d, t, layer] for d in range(PLANE)]
            while len(x) > 1:
                x = [a + b for a, b in zip(x[::2], x[1::2])]
            out[t, layer] = x[0]


def address_kernel(ids, order, mine, other, out):
    out[...] = jnp.zeros_like(out)
    for layer in range(LAYERS):
        @pl.when((order[layer] >> 4) == ids[1])
        def _(layer=layer):
            for t in range(2):
                out[order[layer] & (PLANE - 1), t] = mine[t, layer] + other[t, layer]


def finish_kernel(got, out):
    for t in range(TILES):
        out[:, 128 * t:128 * (t + 1)] = got[t // 2, t % 2]


def vm():
    return pl.BlockSpec(memory_space=pltpu.VMEM)


def sm():
    return pl.BlockSpec(memory_space=pltpu.SMEM)


def shape(*dims):
    return jax.ShapeDtypeStruct(dims, jnp.float32)


def field(rows):
    return shape(rows, 2, 128, 128)


def scr(*dims):
    return pltpu.VMEM(dims, jnp.float32)


def wide(rows):
    return scr(rows, 2, PAD, 128)


def call(kernel, ins, outs, scratch, mib):
    return pl.pallas_call(
        kernel, out_shape=outs, in_specs=ins, out_specs=jax.tree.map(lambda _: vm(), outs),
        scratch_shapes=scratch,
        compiler_params=pltpu.CompilerParams(vmem_limit_bytes=mib << 20),
        cost_estimate=pl.CostEstimate(flops=20_000_000, bytes_accessed=4 << 20, transcendentals=0),
    )


def forward_and_back(angles, depth_order, slices, cotangent):
    n_row = lax.axis_size("row")
    group = lax.axis_index("illum") // PLANE
    ids = jnp.stack([lax.axis_index("row"), group]).astype(jnp.int32)
    groups = [list(range(g * PLANE, (g + 1) * PLANE)) for g in range(2)]
    swap = [(i, (i + PLANE) % (2 * PLANE)) for i in range(2 * PLANE)]

    def meet(x_e, x_o, by):
        even = [(i, i ^ by) for i in range(n_row)]
        odd = [(i, i + by) for i in range(by, n_row - by) if i & by]
        odd = odd + [(j, i) for i, j in odd]
        got_o = lax.ppermute(x_o, "row", odd)
        got_e = lax.ppermute(x_e, "row", even)
        return got_e, got_o

    def exchange(x):
        flat = x.reshape(-1, 128)
        flat = lax.all_to_all(flat, "illum", 0, 0, axis_index_groups=groups, tiled=True)
        return flat.reshape(x.shape)

    def rows_first(x):
        return x.reshape(8, ROWS, TILES, 128).transpose(0, 2, 1, 3).reshape(-1, 128)

    mine = slices[0].reshape(ROWS, TILES, 128).transpose(1, 0, 2)
    other = lax.ppermute(mine, "illum", swap)
    cot_e, cot_o = meet(cotangent, cotangent, 1)
    own, send_e, send_o = call(
        split_kernel, [sm(), vm()], (field(8), field(4), field(4)), [], 6)(
            ids, rows_first(cotangent))
    far_e, far_o = meet(send_e, send_o, 2)
    dealt = call(deal_kernel, [vm()] * 2, shape(PLANE, 2, 2, ROWS, 128), [], 2)(
        mine, other)
    got = exchange(dealt)
    halo_e, halo_o = call(halo_kernel, [vm()] * 2, (field(8),) * 2, [], 6)(
        rows_first(cot_e), rows_first(cot_o))
    whole = call(pick_kernel, [sm(), sm(), vm()], shape(PLANE, 2, LAYERS, ROWS, 128), [],
                 2)(ids, depth_order, got)
    phases = exchange(whole).reshape(-1, 128)
    ph_e, ph_o = meet(phases, phases, 1)

    table = scr(TILES * LAYERS * ROWS, 128)
    w1 = call(adjoint_kernel, [sm()] + [vm()] * 5, field(EXT), [wide(32)] * 4,
              20)(ids, own, halo_e, halo_o, far_e, far_o)
    cos_own, sin_own = call(
        phase_kernel, [vm()], (shape(LAYERS * ROWS, 128, 128),) * 2, [table] * 2,
        5)(phases)
    spreads = scr(LAYERS * EXT, 128, 128)
    terms, last_e, last_o = call(
        main_kernel, [sm()] * 2 + [vm()] * 5,
        (shape(TILES * LAYERS * ROWS, 128), field(4), field(4)),
        [table, table, spreads, spreads, scr(2, 128, 128)] + [wide(EXT)] * 4
        + [scr(16, 2, 128, 128)] + [wide(EXT)] * 3, 40)(
            ids, angles, ph_e, ph_o, cos_own, sin_own, w1)
    parts = exchange(terms).reshape(PLANE, 2, LAYERS, ROWS, 128)
    half = call(sum_kernel, [vm()], shape(2, LAYERS, ROWS, 128), [], 2)(parts)
    half_z = lax.ppermute(half, "illum", swap)
    r_e, r_o = meet(last_e, last_o, 1)
    send = call(address_kernel, [sm(), sm()] + [vm()] * 2, shape(PLANE, 2, ROWS, 128), [],
                2)(ids, depth_order, half, half_z)
    back = exchange(send)
    out = call(exit_kernel, [sm()] + [vm()] * 4, shape(2048, 128),
               [wide(16)] * 4 + [scr(8, 2, 128, 128)], 12)(
                   ids, last_e, last_o, r_e, r_o)
    grad = call(finish_kernel, [vm()], shape(ROWS, COLS), [], 2)(back)
    out = out.reshape(8, TILES, ROWS, 128).transpose(0, 2, 1, 3)
    return out.reshape(cotangent.shape), grad[None]


def solution(mesh):
    placed = (P("illum", None), P(), P("illum", "row", None), P("illum", None, "row", None))
    return jax.shard_map(
        forward_and_back,
        mesh=mesh,
        in_specs=placed,
        out_specs=(P("illum", None, "row", None), P("illum", "row", None)),
        check_vma=False,
    )
```

```python
import math

import jax
import jax.numpy as jnp
from jax import lax
from jax.experimental import pallas as pl
from jax.experimental.pallas import tpu as pltpu
from jax.sharding import PartitionSpec as P


rate_scale = 0.3
ROWS = 8
COLS = 4096
TILES = COLS // 128
LAYERS = 3
HALO = 8
EXT = ROWS + 2 * HALO
N_ROW = 8
NX = ROWS * N_ROW
PAD = 144
PLANE = 16

SIN_C = (0.9999999996397458, -0.16666666036106006, 0.00833331543673961,
         -0.00019839409893936808, 2.7469726872825416e-06, -2.3138942785856126e-08)
COS_C = (0.9999999953627682, -0.49999991881071015, 0.04166643614419552,
         -0.001388649171259302, 2.4688583708756773e-05, -2.5084304017242627e-07)


def horner(coefs, z):
    r = z * coefs[-1] + coefs[-2]
    for c in coefs[-3::-1]:
        r = r * z + c
    return r


def sincos(x):
    y = x * 0.5
    z = y * y
    s = y * horner(SIN_C, z)
    c = horner(COS_C, z)
    s2 = s + s
    return s2 * c, 1.0 - s2 * s


def chunk(j):
    return slice(8 * j, 8 * j + 8)


def padded(j, shift=0):
    return slice(8 + 8 * j + shift, 16 + 8 * j + shift)


def fill_pads(ref, rows):
    flat = ref.reshape(rows * 2 * PAD, 128)
    tile = lax.broadcasted_iota(jnp.int32, (rows * 2, 128), 1) & (TILES - 1)
    high = flat[pl.ds(135, rows * 2, stride=PAD), :]
    low = flat[pl.ds(8, rows * 2, stride=PAD), :]
    flat[pl.ds(7, rows * 2, stride=PAD), :] = jnp.where(tile == 0, 0.0, pltpu.roll(high, 1, 1))
    flat[pl.ds(136, rows * 2, stride=PAD), :] = jnp.where(
        tile == TILES - 1, 0.0, pltpu.roll(low, 127, 1))


def clear_outside(row, ref, base, rows):
    for at in (base - 1 - ROWS * row, base + NX - ROWS * row):
        @pl.when((at >= 0) & (at < rows))
        def _(at=at):
            ref[at] = jnp.zeros((2, PAD, 128), jnp.float32)


def lap_pair(src, r, k, j):
    v = [src[r + q, k, padded(j), :] for q in (-1, 0, 1, 2)]
    out = []
    for q in (0, 1):
        side = src[r + q, k, padded(j, -1), :] + src[r + q, k, padded(j, 1), :]
        out.append((v[q] + v[q + 2]) + side - 4.0 * v[q + 1])
    return out


def step(row, src, rows, base, h, powers, factor, write, outs=()):
    prev = src
    for n, dst in enumerate(powers):
        lo, count = base - h + 1 + n, ROWS + 2 * (h - 1 - n)

        def body(i, _, prev=prev, dst=dst, lo=lo):
            r = lo + 2 * i
            for k in range(2):
                for j in range(16):
                    a, b = lap_pair(prev, r, k, j)
                    dst[r, k, padded(j), :] = a
                    dst[r + 1, k, padded(j), :] = b
            return 0

        lax.fori_loop(0, count // 2, body, 0)
        fill_pads(dst, rows)
        clear_outside(row, dst, base, rows)
        prev = dst
    l1, l2, l3 = powers
    c1, c2, c3, c4 = factor, -factor**2 / 2, -factor**3 / 6, factor**4 / 24
    lo = base - h + 4

    def last(i, _):
        r = lo + 2 * i
        for j in range(16):
            l4 = [lap_pair(l3, r, k, j) for k in range(2)]
            for q in (0, 1):
                even, odd = [], []
                for k in range(2):
                    at = (r + q, k, padded(j), slice(None))
                    even.append(src[at] + (c2 * l2[at] + c4 * l4[k][q]))
                    odd.append(c1 * l1[at] + c3 * l3[at])
                write(r + q, j, even[0] - odd[1], even[1] + odd[0])
        return 0

    pairs = (ROWS + 2 * (h - 4)) // 2
    parts = len(outs) or 1
    for n in range(parts):
        lax.fori_loop(n * pairs // parts, (n + 1) * pairs // parts, last, 0)
        if outs:
            outs[n].start()


def natural(g, k, r):
    return pl.ds((g * 2 + k) * TILES * ROWS + r, TILES, stride=ROWS)


def turned(cot, k, r):
    return jnp.concatenate([cot[natural(g, k, r), :] for g in range(4)], axis=0).T


def split_kernel(ids, cot, out, send_e, send_o, own, sem):
    def body(r, _):
        for k in range(2):
            own[r, k] = turned(cot, k, r)
        return 0

    lax.fori_loop(0, ROWS, body, 0)
    keep = pltpu.make_async_copy(own, out, sem)
    keep.start()
    upper = (ids[0] >> 1) & 1
    for r in range(4):
        send_e[r] = own[r + 4 * (1 - upper)]
        send_o[r] = own[r + 4 * upper]
    keep.wait()


def put(dst, at, src, n):
    def body(r, _):
        for k in range(2):
            dst[at + r, k, 8:136, :] = src[r, k]
        return 0

    lax.fori_loop(0, n, body, 0)


def adjoint_kernel(ids, own, cot_e, cot_o, far_e, far_o, out,
                   own_v, near_e, near_o, res, u, l1, l2, l3, sems):
    row = ids[0]
    odd, upper = row & 1, (row >> 1) & 1
    ins = [
        pltpu.make_async_copy(a, b, sems.at[n])
        for n, (a, b) in enumerate(((cot_e, near_e), (cot_o, near_o), (own, own_v)))
    ]
    for c in ins:
        c.start()
    for c, near, at in ((ins[0], near_e, 20 - 16 * odd), (ins[1], near_o, 4 + 16 * odd)):
        c.wait()

        def turn(r, _, near=near, at=at):
            for k in range(2):
                u[at + r, k, 8:136, :] = turned(near, k, r)
            return 0

        lax.fori_loop(0, ROWS, turn, 0)
    ins[2].wait()
    put(u, 12, own_v, 8)
    put(u, 28 - 28 * upper, far_e, 4)
    put(u, 28 * upper, far_o, 4)
    fill_pads(u, 32)

    def write(r, j, re, im):
        res[r - 4, 0, chunk(j), :] = re
        res[r - 4, 1, chunk(j), :] = im

    outs = [
        pltpu.make_async_copy(res.at[8 * n:8 * n + 8], out.at[8 * n:8 * n + 8], sems.at[3 + n])
        for n in range(3)
    ]
    step(row, u, 32, 12, 12, (l1, l2, l3), -rate_scale, write, outs)
    for c in outs:
        c.wait()


def exit_kernel(ids, sent_e, sent_o, got_e, got_o, out, u, l1, l2, l3, res):
    row = ids[0]
    odd = row & 1
    put(u, 8 - 4 * odd, sent_e, 4)
    put(u, 4 + 4 * odd, sent_o, 4)
    put(u, 12 - 12 * odd, got_e, 4)
    put(u, 12 * odd, got_o, 4)
    fill_pads(u, 16)

    def write(r, j, re, im):
        res[r - 4, 0, chunk(j), :] = re
        res[r - 4, 1, chunk(j), :] = im

    step(row, u, 16, 4, 4, (l1, l2, l3), rate_scale, write)

    def body(r, _):
        for k in range(2):
            x = res[r, k].T
            for g in range(4):
                out[natural(g, k, r), :] = x[g * TILES:(g + 1) * TILES]
        return 0

    lax.fori_loop(0, ROWS, body, 0)


def trig_tables(phases, cos_n, sin_n):
    def body(i, _):
        at = pl.ds(pl.multiple_of(i * 24, 8), 24)
        s, c = sincos(phases[at, :])
        sin_n[at, :] = s
        cos_n[at, :] = c
        return 0

    lax.fori_loop(0, TILES, body, 0)


def spread(ref, n):
    x = ref[pl.ds(n, TILES, stride=LAYERS * ROWS), :]
    return jnp.concatenate([x] * 4, axis=0).T


def phase_kernel(phases, cos_out, sin_out, cos_n, sin_n):
    trig_tables(phases, cos_n, sin_n)

    def body(i, _):
        for n in (2 * i, 2 * i + 1):
            cos_out[n] = spread(cos_n, n)
            sin_out[n] = spread(sin_n, n)
        return 0

    lax.fori_loop(0, LAYERS * ROWS // 2, body, 0)


def main_kernel(ids, angles, ph_e, ph_o, cos_own, sin_own, w1_far,
                terms, last_e, last_o,
                cos_n, sin_n, cosr, sinr, beam, u, v, w, w2, raw, l1, l2, l3, w1, sem):
    row = ids[0]
    odd = row & 1
    fetch = pltpu.make_async_copy(w1_far, w1, sem)
    fetch.start()
    for ph, above in ((ph_e, odd), (ph_o, 1 - odd)):
        trig_tables(ph, cos_n, sin_n)
        first = (HALO + ROWS) * (1 - above)
        for layer in range(LAYERS):
            lo, count = (4 * above, 4) if layer == 1 else (0, 8)

            def body(i, _, layer=layer, first=first, lo=lo):
                for q in range(2):
                    r = lo + 2 * i + q
                    cosr[layer * EXT + first + r] = spread(cos_n, layer * ROWS + r)
                    sinr[layer * EXT + first + r] = spread(sin_n, layer * ROWS + r)
                return 0

            lax.fori_loop(0, count // 2, body, 0)
    for layer in range(LAYERS):
        def copy(r, _, layer=layer):
            cosr[layer * EXT + HALO + r] = cos_own[layer * ROWS + r]
            sinr[layer * EXT + HALO + r] = sin_own[layer * ROWS + r]
            return 0

        lax.fori_loop(0, ROWS, copy, 0)

    lane = lax.broadcasted_iota(jnp.int32, (8, 128), 1)
    sub = lax.broadcasted_iota(jnp.int32, (8, 128), 0)
    beam_of = lane >> 5
    pv, qv = [
        jnp.where(beam_of < 2,
                  jnp.where(beam_of == 0, angles[0, n], angles[1, n]),
                  jnp.where(beam_of == 2, angles[2, n], angles[3, n]))
        for n in range(2)
    ]
    for j in range(16):
        col = (lane & (TILES - 1)) * 128 + sub + 8 * j
        k = (qv * col) & (COLS - 1)
        s, c = sincos((k - COLS // 2).astype(jnp.float32) * (2.0 * math.pi / COLS))
        beam[0, chunk(j), :] = -c
        beam[1, chunk(j), :] = -s

    def phase_at(layer, r, j):
        return cosr[layer * EXT + r, chunk(j), :], sinr[layer * EXT + r, chunk(j), :]

    def incident(r, _):
        k = (pv * (row * ROWS + r - HALO)) & (NX - 1)
        sa, ca = sincos((k - NX // 2).astype(jnp.float32) * (2.0 * math.pi / NX))
        for j in range(16):
            c, s = phase_at(0, r, j)
            a = sa * s - ca * c
            b = -(sa * c + ca * s)
            er, ei = beam[0, chunk(j), :], beam[1, chunk(j), :]
            u[r, 0, padded(j), :] = er * a - ei * b
            u[r, 1, padded(j), :] = ei * a + er * b
        return 0

    lax.fori_loop(0, EXT, incident, 0)
    fill_pads(u, EXT)
    clear_outside(row, u, HALO, EXT)

    def write_v(r, j, re, im):
        c, s = phase_at(1, r, j)
        v[r, 0, padded(j), :] = re * c - im * s
        v[r, 1, padded(j), :] = re * s + im * c

    step(row, u, EXT, HALO, 8, (l1, l2, l3), rate_scale, write_v)
    fill_pads(v, EXT)
    clear_outside(row, v, HALO, EXT)

    def write_last(r, j, re, im):
        c, s = phase_at(2, r, j)
        w2[r, 0, padded(j), :] = re * c - im * s
        w2[r, 1, padded(j), :] = re * s + im * c

    step(row, v, EXT, HALO, 4, (l1, l2, l3), rate_scale, write_last)
    for r in range(4):
        for k in range(2):
            last_e[r, k] = w2[HALO + r + 4 * (1 - odd), k, 8:136, :]
            last_o[r, k] = w2[HALO + r + 4 * odd, k, 8:136, :]

    def term(layer, adjoint, stored):
        def body(i, _):
            for r in (2 * i, 2 * i + 1):
                x = adjoint(r, 1) * stored(r, 0) - adjoint(r, 0) * stored(r, 1)
                x = x.T
                x = (x[:TILES] + x[TILES:2 * TILES]) + (x[2 * TILES:3 * TILES] + x[3 * TILES:])
                terms[pl.ds(layer * ROWS + r, TILES, stride=LAYERS * ROWS), :] = x
            return 0

        lax.fori_loop(0, ROWS // 2, body, 0)

    def own(ref):
        return lambda r, k: ref[HALO + r, k, 8:136, :]

    fetch.wait()
    term(2, lambda r, k: w1[HALO + r, k], own(w2))

    def back(r, _):
        for j in range(16):
            c, s = phase_at(2, r, j)
            re, im = w1[r, 0, chunk(j), :], w1[r, 1, chunk(j), :]
            w[r, 0, padded(j), :] = re * c + im * s
            w[r, 1, padded(j), :] = im * c - re * s
        return 0

    lax.fori_loop(0, EXT, back, 0)
    fill_pads(w, EXT)
    clear_outside(row, w, HALO, EXT)

    def mid(r, j, re, im):
        c, s = phase_at(1, r, j)
        raw[r - 4, 0, chunk(j), :] = re
        raw[r - 4, 1, chunk(j), :] = im
        w2[r, 0, padded(j), :] = re * c + im * s
        w2[r, 1, padded(j), :] = im * c - re * s

    step(row, w, EXT, HALO, 8, (l1, l2, l3), -rate_scale, mid)
    fill_pads(w2, EXT)
    clear_outside(row, w2, HALO, EXT)
    term(1, lambda r, k: raw[r + 4, k], own(v))

    def final(r, j, re, im):
        raw[r - 4, 0, chunk(j), :] = re
        raw[r - 4, 1, chunk(j), :] = im

    step(row, w2, EXT, HALO, 4, (l1, l2, l3), -rate_scale, final)
    term(0, lambda r, k: raw[r + 4, k], own(u))


def deal_kernel(mine, other, out):
    for t in range(TILES):
        out[t // 2, 0, t % 2] = mine[t]
        out[t // 2, 1, t % 2] = other[t]


def pick_kernel(ids, order, got, out):
    for layer in range(LAYERS):
        for t in range(2):
            x = got[order[layer] & (PLANE - 1), (order[layer] >> 4) ^ ids[1], t]
            for d in range(PLANE):
                out[d, t, layer] = x


def sum_kernel(parts, out):
    for layer in range(LAYERS):
        for t in range(2):
            x = [parts[d, t, layer] for d in range(PLANE)]
            while len(x) > 1:
                x = [a + b for a, b in zip(x[::2], x[1::2])]
            out[t, layer] = x[0]


def address_kernel(ids, order, mine, other, out):
    out[...] = jnp.zeros_like(out)
    for layer in range(LAYERS):
        @pl.when((order[layer] >> 4) == ids[1])
        def _(layer=layer):
            for t in range(2):
                out[order[layer] & (PLANE - 1), t] = mine[t, layer] + other[t, layer]


def finish_kernel(got, out):
    for t in range(TILES):
        out[:, 128 * t:128 * (t + 1)] = got[t // 2, t % 2]


def vm():
    return pl.BlockSpec(memory_space=pltpu.VMEM)


def hbm():
    return pl.BlockSpec(memory_space=pltpu.HBM)


def in_hbm(x):
    return pltpu.with_memory_space_constraint(x, pltpu.HBM)


def sm():
    return pl.BlockSpec(memory_space=pltpu.SMEM)


def shape(*dims):
    return jax.ShapeDtypeStruct(dims, jnp.float32)


def field(rows):
    return shape(rows, 2, 128, 128)


def field_hbm(rows):
    return pltpu.HBM((rows, 2, 128, 128), jnp.float32)


def scr(*dims):
    return pltpu.VMEM(dims, jnp.float32)


def wide(rows):
    return scr(rows, 2, PAD, 128)


def call(kernel, ins, outs, scratch, mib, out_specs=None):
    return pl.pallas_call(
        kernel, out_shape=outs, in_specs=ins,
        out_specs=out_specs or jax.tree.map(lambda _: vm(), outs),
        scratch_shapes=scratch,
        compiler_params=pltpu.CompilerParams(vmem_limit_bytes=mib << 20),
        cost_estimate=pl.CostEstimate(flops=20_000_000, bytes_accessed=4 << 20, transcendentals=0),
    )


def forward_and_back(angles, depth_order, slices, cotangent):
    n_row = lax.axis_size("row")
    group = lax.axis_index("illum") // PLANE
    ids = jnp.stack([lax.axis_index("row"), group]).astype(jnp.int32)
    groups = [list(range(g * PLANE, (g + 1) * PLANE)) for g in range(2)]
    swap = [(i, (i + PLANE) % (2 * PLANE)) for i in range(2 * PLANE)]

    def meet(x_e, x_o, by):
        even = [(i, i ^ by) for i in range(n_row)]
        odd = [(i, i + by) for i in range(by, n_row - by) if i & by]
        odd = odd + [(j, i) for i, j in odd]
        got_o = lax.ppermute(x_o, "row", odd)
        got_e = lax.ppermute(x_e, "row", even)
        return got_e, got_o

    def exchange(x):
        flat = x.reshape(-1, 128)
        flat = lax.all_to_all(flat, "illum", 0, 0, axis_index_groups=groups, tiled=True)
        return flat.reshape(x.shape)

    def rows_first(x):
        return x.reshape(8, ROWS, TILES, 128).transpose(0, 2, 1, 3).reshape(-1, 128)

    mine = slices[0].reshape(ROWS, TILES, 128).transpose(1, 0, 2)
    other = lax.ppermute(mine, "illum", swap)
    cot_e, cot_o = meet(cotangent, cotangent, 1)
    own, send_e, send_o = call(
        split_kernel, [sm(), vm()], (field_hbm(8), field(4), field(4)),
        [scr(8, 2, 128, 128), pltpu.SemaphoreType.DMA], 6, (hbm(), vm(), vm()))(
            ids, rows_first(cotangent))
    far_e, far_o = meet(send_e, send_o, 2)
    dealt = call(deal_kernel, [vm()] * 2, shape(PLANE, 2, 2, ROWS, 128), [], 2)(
        mine, other)
    got = exchange(dealt)
    whole = call(pick_kernel, [sm(), sm(), vm()], shape(PLANE, 2, LAYERS, ROWS, 128), [],
                 2)(ids, depth_order, got)
    phases = exchange(whole).reshape(-1, 128)
    ph_e, ph_o = meet(phases, phases, 1)

    table = scr(TILES * LAYERS * ROWS, 128)
    w1 = call(
        adjoint_kernel, [sm()] + [hbm()] * 3 + [vm()] * 2, field_hbm(EXT),
        [scr(8, 2, 128, 128), scr(2048, 128), scr(2048, 128), scr(EXT, 2, 128, 128)]
        + [wide(32)] * 4 + [pltpu.SemaphoreType.DMA((6,))], 27, hbm())(
            ids, *map(in_hbm, (own, rows_first(cot_e), rows_first(cot_o))), far_e, far_o)
    cos_own, sin_own = call(
        phase_kernel, [vm()], (shape(LAYERS * ROWS, 128, 128),) * 2, [table] * 2,
        5)(phases)
    spreads = scr(LAYERS * EXT, 128, 128)
    terms, last_e, last_o = call(
        main_kernel, [sm()] * 2 + [vm()] * 4 + [hbm()],
        (shape(TILES * LAYERS * ROWS, 128), field(4), field(4)),
        [table, table, spreads, spreads, scr(2, 128, 128)] + [wide(EXT)] * 4
        + [scr(16, 2, 128, 128)] + [wide(EXT)] * 3
        + [scr(EXT, 2, 128, 128), pltpu.SemaphoreType.DMA], 43)(
            ids, angles, ph_e, ph_o, cos_own, sin_own, in_hbm(w1))
    parts = exchange(terms).reshape(PLANE, 2, LAYERS, ROWS, 128)
    half = call(sum_kernel, [vm()], shape(2, LAYERS, ROWS, 128), [], 2)(parts)
    half_z = lax.ppermute(half, "illum", swap)
    r_e, r_o = meet(last_e, last_o, 1)
    send = call(address_kernel, [sm(), sm()] + [vm()] * 2, shape(PLANE, 2, ROWS, 128), [],
                2)(ids, depth_order, half, half_z)
    back = exchange(send)
    out = call(exit_kernel, [sm()] + [vm()] * 4, shape(2048, 128),
               [wide(16)] * 4 + [scr(8, 2, 128, 128)], 12)(
                   ids, last_e, last_o, r_e, r_o)
    grad = call(finish_kernel, [vm()], shape(ROWS, COLS), [], 2)(back)
    out = out.reshape(8, TILES, ROWS, 128).transpose(0, 2, 1, 3)
    return out.reshape(cotangent.shape), grad[None]


def solution(mesh):
    placed = (P("illum", None), P(), P("illum", "row", None), P("illum", None, "row", None))
    return jax.shard_map(
        forward_and_back,
        mesh=mesh,
        in_specs=placed,
        out_specs=(P("illum", None, "row", None), P("illum", "row", None)),
        check_vma=False,
    )
```

```python
import functools
import math

import jax
import jax.numpy as jnp
from jax import lax
from jax.experimental import pallas as pl
from jax.experimental.pallas import tpu as pltpu
from jax.sharding import PartitionSpec as P


rate_scale = 0.3
ROWS = 8
COLS = 4096
TILES = COLS // 128
LAYERS = 3
HALO = 8
EXT = ROWS + 2 * HALO
N_ROW = 8
NX = ROWS * N_ROW
PAD = 144
PLANE = 16

SIN_C = (0.9999999996397458, -0.16666666036106006, 0.00833331543673961,
         -0.00019839409893936808, 2.7469726872825416e-06, -2.3138942785856126e-08)
COS_C = (0.9999999953627682, -0.49999991881071015, 0.04166643614419552,
         -0.001388649171259302, 2.4688583708756773e-05, -2.5084304017242627e-07)


def horner(coefs, z):
    r = z * coefs[-1] + coefs[-2]
    for c in coefs[-3::-1]:
        r = r * z + c
    return r


def sincos(x):
    y = x * 0.5
    z = y * y
    s = y * horner(SIN_C, z)
    c = horner(COS_C, z)
    s2 = s + s
    return s2 * c, 1.0 - s2 * s


def chunk(j):
    return slice(8 * j, 8 * j + 8)


def padded(j, shift=0):
    return slice(8 + 8 * j + shift, 16 + 8 * j + shift)


def fill_pads(ref, rows):
    flat = ref.reshape(rows * 2 * PAD, 128)
    tile = lax.broadcasted_iota(jnp.int32, (rows * 2, 128), 1) & (TILES - 1)
    high = flat[pl.ds(135, rows * 2, stride=PAD), :]
    low = flat[pl.ds(8, rows * 2, stride=PAD), :]
    flat[pl.ds(7, rows * 2, stride=PAD), :] = jnp.where(tile == 0, 0.0, pltpu.roll(high, 1, 1))
    flat[pl.ds(136, rows * 2, stride=PAD), :] = jnp.where(
        tile == TILES - 1, 0.0, pltpu.roll(low, 127, 1))


def clear_outside(row, ref, base, rows):
    for at in (base - 1 - ROWS * row, base + NX - ROWS * row):
        @pl.when((at >= 0) & (at < rows))
        def _(at=at):
            ref[at] = jnp.zeros((2, PAD, 128), jnp.float32)


def lap_pair(src, r, k, j):
    v = [src[r + q, k, padded(j), :] for q in (-1, 0, 1, 2)]
    out = []
    for q in (0, 1):
        side = src[r + q, k, padded(j, -1), :] + src[r + q, k, padded(j, 1), :]
        out.append((v[q] + v[q + 2]) + side - 4.0 * v[q + 1])
    return out


def step(row, src, rows, base, h, powers, factor, write):
    prev = src
    for n, dst in enumerate(powers):
        lo, count = base - h + 1 + n, ROWS + 2 * (h - 1 - n)

        def body(i, _, prev=prev, dst=dst, lo=lo):
            r = lo + 2 * i
            for k in range(2):
                for j in range(16):
                    pair = lap_pair(prev, r, k, j)
                    for q in (0, 1):
                        dst[r + q, k, padded(j), :] = pair[q]
            return 0

        lax.fori_loop(0, count // 2, body, 0)
        fill_pads(dst, rows)
        clear_outside(row, dst, base, rows)
        prev = dst
    l1, l2, l3 = powers
    c1, c2, c3, c4 = factor, -factor**2 / 2, -factor**3 / 6, factor**4 / 24
    lo = base - h + 4

    def last(i, _):
        r = lo + 2 * i
        for j in range(16):
            l4 = [lap_pair(l3, r, k, j) for k in range(2)]
            for q in (0, 1):
                even, odd = [], []
                for k in range(2):
                    at = (r + q, k, padded(j), slice(None))
                    even.append(src[at] + (c2 * l2[at] + c4 * l4[k][q]))
                    odd.append(c1 * l1[at] + c3 * l3[at])
                write(r + q, j, even[0] - odd[1], even[1] + odd[0])
        return 0

    lax.fori_loop(0, (ROWS + 2 * (h - 4)) // 2, last, 0)


def natural(g, k, r):
    return pl.ds((g * 2 + k) * TILES * ROWS + r, TILES, stride=ROWS)


def turned(cot, k, r):
    return jnp.concatenate([cot[natural(g, k, r), :] for g in range(4)], axis=0).T


def split_kernel(ids, cot, out, send_e, send_o, own, sem):
    def body(r, _):
        for k in range(2):
            own[r, k] = turned(cot, k, r)
        return 0

    lax.fori_loop(0, ROWS, body, 0)
    keep = pltpu.make_async_copy(own, out, sem)
    keep.start()
    odd = ids[0] & 1
    for r in range(4):
        send_e[r] = own[r + 4 * (1 - odd)]
        send_o[r] = own[r + 4 * odd]
    keep.wait()


def put(dst, at, src, n):
    def body(r, _):
        for k in range(2):
            dst[at + r, k, 8:136, :] = src[r, k]
        return 0

    lax.fori_loop(0, n, body, 0)


def adjoint_kernel(ids, own, got_e, got_o, out, own_v, res, u, l1, l2, l3, sem):
    row = ids[0]
    odd = row & 1
    fetch = pltpu.make_async_copy(own, own_v, sem)
    fetch.start()
    put(u, 12 - 12 * odd, got_e, 4)
    put(u, 12 * odd, got_o, 4)
    fetch.wait()
    put(u, 4, own_v, 8)
    fill_pads(u, 16)

    def write(r, j, re, im):
        res[r - 4, 0, chunk(j), :] = re
        res[r - 4, 1, chunk(j), :] = im

    step(row, u, 16, 4, 4, (l1, l2, l3), -rate_scale, write)
    give = pltpu.make_async_copy(res, out, sem)
    give.start()
    give.wait()


def exit_kernel(ids, sent_e, sent_o, got_e, got_o, out, u, l1, l2, l3, res):
    row = ids[0]
    odd = row & 1
    put(u, 8 - 4 * odd, sent_e, 4)
    put(u, 4 + 4 * odd, sent_o, 4)
    put(u, 12 - 12 * odd, got_e, 4)
    put(u, 12 * odd, got_o, 4)
    fill_pads(u, 16)

    def write(r, j, re, im):
        res[r - 4, 0, chunk(j), :] = re
        res[r - 4, 1, chunk(j), :] = im

    step(row, u, 16, 4, 4, (l1, l2, l3), rate_scale, write)

    def body(r, _):
        for k in range(2):
            x = res[r, k].T
            for g in range(4):
                out[natural(g, k, r), :] = x[g * TILES:(g + 1) * TILES]
        return 0

    lax.fori_loop(0, ROWS, body, 0)


def trig_tables(phases, cos_n, sin_n):
    def body(i, _):
        at = pl.ds(pl.multiple_of(i * 48, 8), 48)
        s, c = sincos(phases[at, :])
        sin_n[at, :] = s
        cos_n[at, :] = c
        return 0

    lax.fori_loop(0, TILES // 2, body, 0)


def spread(ref, n):
    x = ref[pl.ds(n, TILES, stride=LAYERS * ROWS), :]
    return jnp.concatenate([x] * 4, axis=0).T


def phase_kernel(phases, cos_out, sin_out, cos_n, sin_n):
    trig_tables(phases, cos_n, sin_n)

    def body(i, _):
        for n in (2 * i, 2 * i + 1):
            cos_out[n] = spread(cos_n, n)
            sin_out[n] = spread(sin_n, n)
        return 0

    lax.fori_loop(0, LAYERS * ROWS // 2, body, 0)


def forward_kernel(ids, angles, ph_e, ph_o, cos_own, sin_own,
                   cosr, sinr, keep0, keep1, keep2, last_e, last_o,
                   cos_n, sin_n, beam, u, v, l1, l2, l3):
    row = ids[0]
    odd = row & 1
    for ph, above in ((ph_e, odd), (ph_o, 1 - odd)):
        trig_tables(ph, cos_n, sin_n)
        first = (HALO + ROWS) * (1 - above)
        for layer in range(LAYERS):
            lo, count = (4 * above, 4) if layer == 1 else (0, 8)

            def body(i, _, layer=layer, first=first, lo=lo):
                for q in range(2):
                    r = lo + 2 * i + q
                    cosr[layer * EXT + first + r] = spread(cos_n, layer * ROWS + r)
                    sinr[layer * EXT + first + r] = spread(sin_n, layer * ROWS + r)
                return 0

            lax.fori_loop(0, count // 2, body, 0)
    for layer in range(LAYERS):
        def copy(r, _, layer=layer):
            cosr[layer * EXT + HALO + r] = cos_own[layer * ROWS + r]
            sinr[layer * EXT + HALO + r] = sin_own[layer * ROWS + r]
            return 0

        lax.fori_loop(0, ROWS, copy, 0)

    lane = lax.broadcasted_iota(jnp.int32, (8, 128), 1)
    sub = lax.broadcasted_iota(jnp.int32, (8, 128), 0)
    beam_of = lane >> 5
    pv, qv = [
        jnp.where(beam_of < 2,
                  jnp.where(beam_of == 0, angles[0, n], angles[1, n]),
                  jnp.where(beam_of == 2, angles[2, n], angles[3, n]))
        for n in range(2)
    ]
    for j in range(16):
        col = (lane & (TILES - 1)) * 128 + sub + 8 * j
        k = (qv * col) & (COLS - 1)
        s, c = sincos((k - COLS // 2).astype(jnp.float32) * (2.0 * math.pi / COLS))
        beam[0, chunk(j), :] = -c
        beam[1, chunk(j), :] = -s

    phase_at = functools.partial(rotation, cosr, sinr)

    def incident(r, _):
        k = (pv * (row * ROWS + r - HALO)) & (NX - 1)
        sa, ca = sincos((k - NX // 2).astype(jnp.float32) * (2.0 * math.pi / NX))
        for j in range(16):
            c, s = phase_at(0, r, j)
            a = sa * s - ca * c
            b = -(sa * c + ca * s)
            er, ei = beam[0, chunk(j), :], beam[1, chunk(j), :]
            u[r, 0, padded(j), :] = er * a - ei * b
            u[r, 1, padded(j), :] = ei * a + er * b
        return 0

    lax.fori_loop(0, EXT, incident, 0)
    fill_pads(u, EXT)
    clear_outside(row, u, HALO, EXT)

    def write_v(r, j, re, im):
        c, s = phase_at(1, r, j)
        v[r, 0, padded(j), :] = re * c - im * s
        v[r, 1, padded(j), :] = re * s + im * c

    step(row, u, EXT, HALO, 8, (l1, l2, l3), rate_scale, write_v)
    fill_pads(v, EXT)
    clear_outside(row, v, HALO, EXT)

    def write_last(r, j, re, im):
        c, s = phase_at(2, r, j)
        keep2[r - HALO, 0, chunk(j), :] = re * c - im * s
        keep2[r - HALO, 1, chunk(j), :] = re * s + im * c

    step(row, v, EXT, HALO, 4, (l1, l2, l3), rate_scale, write_last)

    def keep(r, _):
        for k in range(2):
            keep0[r, k] = u[HALO + r, k, 8:136, :]
            keep1[r, k] = v[HALO + r, k, 8:136, :]
        return 0

    lax.fori_loop(0, ROWS, keep, 0)
    for r in range(4):
        last_e[r] = keep2[r + 4 * (1 - odd)]
        last_o[r] = keep2[r + 4 * odd]


def rotation(cosr, sinr, layer, r, j):
    return cosr[layer * EXT + r, chunk(j), :], sinr[layer * EXT + r, chunk(j), :]


def back_kernel(ids, cosr, sinr, keep0, keep1, keep2, w1, w_e, w_o, terms,
                w, w2, raw, l1, l2, l3):
    row = ids[0]
    odd = row & 1
    phase_at = functools.partial(rotation, cosr, sinr)

    def term(layer, adjoint, stored):
        def body(i, _):
            for r in (2 * i, 2 * i + 1):
                x = adjoint(r, 1) * stored(r, 0) - adjoint(r, 0) * stored(r, 1)
                x = x.T
                x = (x[:TILES] + x[TILES:2 * TILES]) + (x[2 * TILES:3 * TILES] + x[3 * TILES:])
                terms[pl.ds(layer * ROWS + r, TILES, stride=LAYERS * ROWS), :] = x
            return 0

        lax.fori_loop(0, ROWS // 2, body, 0)

    def of(ref, at=0):
        return lambda r, k: ref[at + r, k]

    for src, at in ((w1, HALO), (w_e, 16 - 16 * odd), (w_o, 16 * odd)):
        def back(r, _, src=src, at=at):
            for j in range(16):
                c, s = phase_at(2, at + r, j)
                re, im = src[r, 0, chunk(j), :], src[r, 1, chunk(j), :]
                w[at + r, 0, padded(j), :] = re * c + im * s
                w[at + r, 1, padded(j), :] = im * c - re * s
            return 0

        lax.fori_loop(0, ROWS, back, 0)
    term(2, of(w1), of(keep2))
    fill_pads(w, EXT)
    clear_outside(row, w, HALO, EXT)

    def mid(r, j, re, im):
        c, s = phase_at(1, r, j)
        raw[r - 4, 0, chunk(j), :] = re
        raw[r - 4, 1, chunk(j), :] = im
        w2[r, 0, padded(j), :] = re * c + im * s
        w2[r, 1, padded(j), :] = im * c - re * s

    step(row, w, EXT, HALO, 8, (l1, l2, l3), -rate_scale, mid)
    fill_pads(w2, EXT)
    clear_outside(row, w2, HALO, EXT)
    term(1, of(raw, 4), of(keep1))

    def final(r, j, re, im):
        raw[r - 4, 0, chunk(j), :] = re
        raw[r - 4, 1, chunk(j), :] = im

    step(row, w2, EXT, HALO, 4, (l1, l2, l3), -rate_scale, final)
    term(0, of(raw, 4), of(keep0))


def pick_kernel(ids, got, out):
    for layer in range(LAYERS):
        for t in range(2):
            x = got[ids[2 + layer], t]
            for d in range(PLANE):
                out[d, t, layer] = x


def gather_kernel(ids, parts, out):
    out[...] = jnp.zeros_like(out)
    for layer in range(LAYERS):
        for t in range(2):
            x = [parts[d, t, layer] for d in range(PLANE)]
            while len(x) > 1:
                x = [a + b for a, b in zip(x[::2], x[1::2])]
            out[ids[2 + layer], t] = x[0]


def finish_kernel(got, out):
    for t in range(TILES):
        out[:, 128 * t:128 * (t + 1)] = got[t // 2, t % 2] + got[PLANE + t // 2, t % 2]


def vm():
    return pl.BlockSpec(memory_space=pltpu.VMEM)


def hbm():
    return pl.BlockSpec(memory_space=pltpu.HBM)


def in_hbm(x):
    return pltpu.with_memory_space_constraint(x, pltpu.HBM)


def sm():
    return pl.BlockSpec(memory_space=pltpu.SMEM)


def shape(*dims):
    return jax.ShapeDtypeStruct(dims, jnp.float32)


def field(rows):
    return shape(rows, 2, 128, 128)


def field_hbm(rows):
    return pltpu.HBM((rows, 2, 128, 128), jnp.float32)


def scr(*dims):
    return pltpu.VMEM(dims, jnp.float32)


def wide(rows):
    return scr(rows, 2, PAD, 128)


def call(kernel, ins, outs, scratch, mib, out_specs=None):
    return pl.pallas_call(
        kernel, out_shape=outs, in_specs=ins,
        out_specs=out_specs or jax.tree.map(lambda _: vm(), outs),
        scratch_shapes=scratch,
        compiler_params=pltpu.CompilerParams(vmem_limit_bytes=mib << 20),
        cost_estimate=pl.CostEstimate(flops=20_000_000, bytes_accessed=4 << 20, transcendentals=0),
    )


def forward_and_back(angles, depth_order, slices, cotangent):
    n_row = lax.axis_size("row")
    group = lax.axis_index("illum") // PLANE
    ids = jnp.concatenate(
        [jnp.stack([lax.axis_index("row"), group]).astype(jnp.int32), depth_order])
    groups = [list(range(g * PLANE, (g + 1) * PLANE)) for g in range(2)]

    def meet(x_e, x_o, by):
        even = [(i, i ^ by) for i in range(n_row)]
        odd = [(i, i + by) for i in range(by, n_row - by) if i & by]
        odd = odd + [(j, i) for i, j in odd]
        got_o = lax.ppermute(x_o, "row", odd)
        got_e = lax.ppermute(x_e, "row", even)
        return got_e, got_o

    def exchange(x, groups=groups):
        flat = x.reshape(-1, 128)
        flat = lax.all_to_all(flat, "illum", 0, 0, axis_index_groups=groups, tiled=True)
        return flat.reshape(x.shape)

    def rows_first(x):
        return x.reshape(8, ROWS, TILES, 128).transpose(0, 2, 1, 3).reshape(-1, 128)

    mine = slices[0].reshape(ROWS, TILES, 128).transpose(1, 0, 2)
    dealt = jnp.broadcast_to(mine[None], (2, TILES, ROWS, 128))
    dealt = dealt.reshape(2 * PLANE, 2, ROWS, 128)
    got = exchange(dealt, None)
    own, send_e, send_o = call(
        split_kernel, [sm(), vm()], (field_hbm(8), field(4), field(4)),
        [scr(8, 2, 128, 128), pltpu.SemaphoreType.DMA], 6, (hbm(), vm(), vm()))(
            ids, rows_first(cotangent))
    cot_e, cot_o = meet(send_e, send_o, 1)
    whole = call(pick_kernel, [sm(), vm()], shape(PLANE, 2, LAYERS, ROWS, 128), [],
                 2)(ids, got)
    phases = exchange(whole).reshape(-1, 128)
    w1 = call(
        adjoint_kernel, [sm(), hbm()] + [vm()] * 2, field_hbm(8),
        [scr(8, 2, 128, 128)] * 2 + [wide(16)] * 4 + [pltpu.SemaphoreType.DMA],
        14, hbm())(ids, in_hbm(own), cot_e, cot_o)
    ph_e, ph_o = meet(phases, phases, 1)
    w_e, w_o = meet(w1, w1, 1)

    table = scr(TILES * LAYERS * ROWS, 128)
    cos_own, sin_own = call(
        phase_kernel, [vm()], (shape(LAYERS * ROWS, 128, 128),) * 2, [table] * 2,
        5)(phases)
    *kept, last_e, last_o = call(
        forward_kernel, [sm()] * 2 + [vm()] * 4,
        (shape(LAYERS * EXT, 128, 128),) * 2 + (field(8),) * 3 + (field(4),) * 2,
        [table, table, scr(2, 128, 128)] + [wide(EXT)] * 5, 20)(
            ids, angles, ph_e, ph_o, cos_own, sin_own)
    terms = call(
        back_kernel, [sm()] + [vm()] * 8, shape(TILES * LAYERS * ROWS, 128),
        [wide(EXT)] * 2 + [scr(16, 2, 128, 128)] + [wide(EXT)] * 3, 21)(
            ids, *kept, w1, w_e, w_o)
    parts = exchange(terms).reshape(PLANE, 2, LAYERS, ROWS, 128)
    r_e, r_o = meet(last_e, last_o, 1)
    send = call(gather_kernel, [sm(), vm()], shape(2 * PLANE, 2, ROWS, 128), [],
                2)(ids, parts)
    back = exchange(send, None)
    out = call(exit_kernel, [sm()] + [vm()] * 4, shape(2048, 128),
               [wide(16)] * 4 + [scr(8, 2, 128, 128)], 12)(
                   ids, last_e, last_o, r_e, r_o)
    grad = call(finish_kernel, [vm()], shape(ROWS, COLS), [], 2)(back)
    out = out.reshape(8, TILES, ROWS, 128).transpose(0, 2, 1, 3)
    return out.reshape(cotangent.shape), grad[None]


def solution(mesh):
    placed = (P("illum", None), P(), P("illum", "row", None), P("illum", None, "row", None))
    return jax.shard_map(
        forward_and_back,
        mesh=mesh,
        in_specs=placed,
        out_specs=(P("illum", None, "row", None), P("illum", "row", None)),
        check_vma=False,
    )
```

```python
import functools
import math

import jax
import jax.numpy as jnp
from jax import lax
from jax.experimental import pallas as pl
from jax.experimental.pallas import tpu as pltpu
from jax.sharding import PartitionSpec as P


rate_scale = 0.3
ROWS = 8
COLS = 4096
TILES = COLS // 128
LAYERS = 3
HALO = 8
EXT = ROWS + 2 * HALO
N_ROW = 8
NX = ROWS * N_ROW
PAD = 144
PLANE = 16

SIN_C = (0.9999999996397458, -0.16666666036106006, 0.00833331543673961,
         -0.00019839409893936808, 2.7469726872825416e-06, -2.3138942785856126e-08)
COS_C = (0.9999999953627682, -0.49999991881071015, 0.04166643614419552,
         -0.001388649171259302, 2.4688583708756773e-05, -2.5084304017242627e-07)


def horner(coefs, z):
    r = z * coefs[-1] + coefs[-2]
    for c in coefs[-3::-1]:
        r = r * z + c
    return r


def sincos(x):
    y = x * 0.5
    z = y * y
    s = y * horner(SIN_C, z)
    c = horner(COS_C, z)
    s2 = s + s
    return s2 * c, 1.0 - s2 * s


def chunk(j):
    return slice(8 * j, 8 * j + 8)


def padded(j, shift=0):
    return slice(8 + 8 * j + shift, 16 + 8 * j + shift)


def fill_pads(ref, rows):
    flat = ref.reshape(rows * 2 * PAD, 128)
    tile = lax.broadcasted_iota(jnp.int32, (rows * 2, 128), 1) & (TILES - 1)
    high = flat[pl.ds(135, rows * 2, stride=PAD), :]
    low = flat[pl.ds(8, rows * 2, stride=PAD), :]
    flat[pl.ds(7, rows * 2, stride=PAD), :] = jnp.where(tile == 0, 0.0, pltpu.roll(high, 1, 1))
    flat[pl.ds(136, rows * 2, stride=PAD), :] = jnp.where(
        tile == TILES - 1, 0.0, pltpu.roll(low, 127, 1))


def clear_outside(row, ref, base, rows):
    for at in (base - 1 - ROWS * row, base + NX - ROWS * row):
        @pl.when((at >= 0) & (at < rows))
        def _(at=at):
            ref[at] = jnp.zeros((2, PAD, 128), jnp.float32)


def lap_rows(src, r, n, k, j):
    v = [src[r + q, k, padded(j), :] for q in range(-1, n + 1)]
    out = []
    for q in range(n):
        side = src[r + q, k, padded(j, -1), :] + src[r + q, k, padded(j, 1), :]
        out.append((v[q] + v[q + 2]) + side - 4.0 * v[q + 1])
    return out


def step(row, src, rows, base, h, powers, factor, write):
    prev = src
    for n, dst in enumerate(powers):
        lo, count = base - h + 1 + n, ROWS + 2 * (h - 1 - n)

        def body(r, n, prev=prev, dst=dst):
            for k in range(2):
                for j in range(16):
                    for q, x in enumerate(lap_rows(prev, r, n, k, j)):
                        dst[r + q, k, padded(j), :] = x

        def four(i, _, body=body, lo=lo):
            body(lo + 4 * i, 4)
            return 0

        lax.fori_loop(0, count // 4, four, 0)
        if count % 4:
            body(lo + count - 2, 2)
        fill_pads(dst, rows)
        clear_outside(row, dst, base, rows)
        prev = dst
    l1, l2, l3 = powers
    c1, c2, c3, c4 = factor, -factor**2 / 2, -factor**3 / 6, factor**4 / 24
    lo = base - h + 4

    def last(i, _):
        r = lo + 2 * i
        for j in range(16):
            l4 = [lap_rows(l3, r, 2, k, j) for k in range(2)]
            for q in (0, 1):
                even, odd = [], []
                for k in range(2):
                    at = (r + q, k, padded(j), slice(None))
                    even.append(src[at] + (c2 * l2[at] + c4 * l4[k][q]))
                    odd.append(c1 * l1[at] + c3 * l3[at])
                write(r + q, j, even[0] - odd[1], even[1] + odd[0])
        return 0

    lax.fori_loop(0, (ROWS + 2 * (h - 4)) // 2, last, 0)


def natural(g, k, r):
    return pl.ds((g * 2 + k) * TILES * ROWS + r, TILES, stride=ROWS)


def turned(cot, k, r):
    return jnp.concatenate([cot[natural(g, k, r), :] for g in range(4)], axis=0).T


def split_kernel(ids, cot, out, send_e, send_o, own, sem):
    def body(r, _):
        for k in range(2):
            own[r, k] = turned(cot, k, r)
        return 0

    lax.fori_loop(0, ROWS, body, 0)
    keep = pltpu.make_async_copy(own, out, sem)
    keep.start()
    odd = ids[0] & 1
    for r in range(4):
        send_e[r] = own[r + 4 * (1 - odd)]
        send_o[r] = own[r + 4 * odd]
    keep.wait()


def put(dst, at, src, n):
    def body(r, _):
        for k in range(2):
            dst[at + r, k, 8:136, :] = src[r, k]
        return 0

    lax.fori_loop(0, n, body, 0)


def adjoint_kernel(ids, own, got_e, got_o, out, own_v, res, u, l1, l2, l3, sem):
    row = ids[0]
    odd = row & 1
    fetch = pltpu.make_async_copy(own, own_v, sem)
    fetch.start()
    put(u, 12 - 12 * odd, got_e, 4)
    put(u, 12 * odd, got_o, 4)
    fetch.wait()
    put(u, 4, own_v, 8)
    fill_pads(u, 16)

    def write(r, j, re, im):
        res[r - 4, 0, chunk(j), :] = re
        res[r - 4, 1, chunk(j), :] = im

    step(row, u, 16, 4, 4, (l1, l2, l3), -rate_scale, write)
    give = pltpu.make_async_copy(res, out, sem)
    give.start()
    give.wait()


def exit_kernel(ids, sent_e, sent_o, got_e, got_o, out, u, l1, l2, l3, res, held, sems):
    row = ids[0]
    odd = row & 1
    fetch = [
        pltpu.make_async_copy(src, held.at[n], sems.at[n])
        for n, src in enumerate((sent_e, sent_o))
    ]
    for c in fetch:
        c.start()
    put(u, 12 - 12 * odd, got_e, 4)
    put(u, 12 * odd, got_o, 4)
    fetch[0].wait()
    put(u, 8 - 4 * odd, held.at[0], 4)
    fetch[1].wait()
    put(u, 4 + 4 * odd, held.at[1], 4)
    fill_pads(u, 16)

    def write(r, j, re, im):
        res[r - 4, 0, chunk(j), :] = re
        res[r - 4, 1, chunk(j), :] = im

    step(row, u, 16, 4, 4, (l1, l2, l3), rate_scale, write)

    def body(r, _):
        for k in range(2):
            x = res[r, k].T
            for g in range(4):
                out[natural(g, k, r), :] = x[g * TILES:(g + 1) * TILES]
        return 0

    lax.fori_loop(0, ROWS, body, 0)


def trig_tables(phases, cos_n, sin_n):
    def body(i, _):
        at = pl.ds(pl.multiple_of(i * 48, 8), 48)
        s, c = sincos(phases[at, :])
        sin_n[at, :] = s
        cos_n[at, :] = c
        return 0

    lax.fori_loop(0, TILES // 2, body, 0)


def spread(ref, n):
    x = ref[pl.ds(n, TILES, stride=LAYERS * ROWS), :]
    return jnp.concatenate([x] * 4, axis=0).T


def phase_kernel(phases, cos_out, sin_out, cos_n, sin_n):
    trig_tables(phases, cos_n, sin_n)

    def body(i, _):
        for n in (2 * i, 2 * i + 1):
            cos_out[n] = spread(cos_n, n)
            sin_out[n] = spread(sin_n, n)
        return 0

    lax.fori_loop(0, LAYERS * ROWS // 2, body, 0)


def forward_kernel(ids, angles, ph_e, ph_o, cos_own, sin_own,
                   cosr, sinr, keep0, keep1, keep2, last_e, last_o,
                   cos_n, sin_n, beam, u, v, l1, l2, l3, sems):
    row = ids[0]
    odd = row & 1
    for ph, above in ((ph_e, odd), (ph_o, 1 - odd)):
        trig_tables(ph, cos_n, sin_n)
        first = (HALO + ROWS) * (1 - above)
        for layer in range(LAYERS):
            lo, count = (4 * above, 4) if layer == 1 else (0, 8)

            def body(i, _, layer=layer, first=first, lo=lo):
                for q in range(2):
                    r = lo + 2 * i + q
                    cosr[layer * EXT + first + r] = spread(cos_n, layer * ROWS + r)
                    sinr[layer * EXT + first + r] = spread(sin_n, layer * ROWS + r)
                return 0

            lax.fori_loop(0, count // 2, body, 0)
    for layer in range(LAYERS):
        def copy(r, _, layer=layer):
            cosr[layer * EXT + HALO + r] = cos_own[layer * ROWS + r]
            sinr[layer * EXT + HALO + r] = sin_own[layer * ROWS + r]
            return 0

        lax.fori_loop(0, ROWS, copy, 0)

    lane = lax.broadcasted_iota(jnp.int32, (8, 128), 1)
    sub = lax.broadcasted_iota(jnp.int32, (8, 128), 0)
    beam_of = lane >> 5
    pv, qv = [
        jnp.where(beam_of < 2,
                  jnp.where(beam_of == 0, angles[0, n], angles[1, n]),
                  jnp.where(beam_of == 2, angles[2, n], angles[3, n]))
        for n in range(2)
    ]
    for j in range(16):
        col = (lane & (TILES - 1)) * 128 + sub + 8 * j
        k = (qv * col) & (COLS - 1)
        s, c = sincos((k - COLS // 2).astype(jnp.float32) * (2.0 * math.pi / COLS))
        beam[0, chunk(j), :] = -c
        beam[1, chunk(j), :] = -s

    phase_at = functools.partial(rotation, cosr, sinr)

    def incident(i, _):
        for r in (2 * i, 2 * i + 1):
            k = (pv * (row * ROWS + r - HALO)) & (NX - 1)
            sa, ca = sincos((k - NX // 2).astype(jnp.float32) * (2.0 * math.pi / NX))
            for j in range(16):
                c, s = phase_at(0, r, j)
                a = sa * s - ca * c
                b = -(sa * c + ca * s)
                er, ei = beam[0, chunk(j), :], beam[1, chunk(j), :]
                u[r, 0, padded(j), :] = er * a - ei * b
                u[r, 1, padded(j), :] = ei * a + er * b
        return 0

    lax.fori_loop(0, EXT // 2, incident, 0)
    fill_pads(u, EXT)
    clear_outside(row, u, HALO, EXT)

    def write_v(r, j, re, im):
        c, s = phase_at(1, r, j)
        v[r, 0, padded(j), :] = re * c - im * s
        v[r, 1, padded(j), :] = re * s + im * c

    step(row, u, EXT, HALO, 8, (l1, l2, l3), rate_scale, write_v)
    fill_pads(v, EXT)
    clear_outside(row, v, HALO, EXT)

    def write_last(r, j, re, im):
        c, s = phase_at(2, r, j)
        keep2[r - HALO, 0, chunk(j), :] = re * c - im * s
        keep2[r - HALO, 1, chunk(j), :] = re * s + im * c

    step(row, v, EXT, HALO, 4, (l1, l2, l3), rate_scale, write_last)
    give = [
        pltpu.make_async_copy(keep2.at[pl.ds(at, 4)], dst, sems.at[n])
        for n, (at, dst) in enumerate(((4 * (1 - odd), last_e), (4 * odd, last_o)))
    ]
    for c in give:
        c.start()

    def keep(r, _):
        for k in range(2):
            keep0[r, k] = u[HALO + r, k, 8:136, :]
            keep1[r, k] = v[HALO + r, k, 8:136, :]
        return 0

    lax.fori_loop(0, ROWS, keep, 0)
    for c in give:
        c.wait()


def rotation(cosr, sinr, layer, r, j):
    return cosr[layer * EXT + r, chunk(j), :], sinr[layer * EXT + r, chunk(j), :]


def back_kernel(ids, cosr, sinr, keep0, keep1, keep2, w1, w_e, w_o, terms,
                w, w2, raw, l1, l2, l3):
    row = ids[0]
    odd = row & 1
    phase_at = functools.partial(rotation, cosr, sinr)

    def term(layer, adjoint, stored):
        def body(i, _):
            for r in (2 * i, 2 * i + 1):
                x = adjoint(r, 1) * stored(r, 0) - adjoint(r, 0) * stored(r, 1)
                x = x.T
                x = (x[:TILES] + x[TILES:2 * TILES]) + (x[2 * TILES:3 * TILES] + x[3 * TILES:])
                terms[pl.ds(layer * ROWS + r, TILES, stride=LAYERS * ROWS), :] = x
            return 0

        lax.fori_loop(0, ROWS // 2, body, 0)

    def of(ref, at=0):
        return lambda r, k: ref[at + r, k]

    for src, at in ((w1, HALO), (w_e, 16 - 16 * odd), (w_o, 16 * odd)):
        def back(r, _, src=src, at=at):
            for j in range(16):
                c, s = phase_at(2, at + r, j)
                re, im = src[r, 0, chunk(j), :], src[r, 1, chunk(j), :]
                w[at + r, 0, padded(j), :] = re * c + im * s
                w[at + r, 1, padded(j), :] = im * c - re * s
            return 0

        lax.fori_loop(0, ROWS, back, 0)
    term(2, of(w1), of(keep2))
    fill_pads(w, EXT)
    clear_outside(row, w, HALO, EXT)

    def mid(r, j, re, im):
        c, s = phase_at(1, r, j)
        raw[r - 4, 0, chunk(j), :] = re
        raw[r - 4, 1, chunk(j), :] = im
        w2[r, 0, padded(j), :] = re * c + im * s
        w2[r, 1, padded(j), :] = im * c - re * s

    step(row, w, EXT, HALO, 8, (l1, l2, l3), -rate_scale, mid)
    fill_pads(w2, EXT)
    clear_outside(row, w2, HALO, EXT)
    term(1, of(raw, 4), of(keep1))

    def final(r, j, re, im):
        raw[r - 4, 0, chunk(j), :] = re
        raw[r - 4, 1, chunk(j), :] = im

    step(row, w2, EXT, HALO, 4, (l1, l2, l3), -rate_scale, final)
    term(0, of(raw, 4), of(keep0))


def double_kernel(mine, out, held, sems):
    fetch = pltpu.make_async_copy(mine, held, sems.at[0])
    fetch.start()
    fetch.wait()
    give = [pltpu.make_async_copy(held, out.at[n], sems.at[n]) for n in range(2)]
    for c in give:
        c.start()
    for c in give:
        c.wait()


def pick_kernel(ids, got, out):
    for layer in range(LAYERS):
        for t in range(2):
            x = got[ids[2 + layer], t]
            for d in range(PLANE):
                out[d, t, layer] = x


def gather_kernel(ids, parts, out):
    out[...] = jnp.zeros_like(out)
    for layer in range(LAYERS):
        for t in range(2):
            x = [parts[d, t, layer] for d in range(PLANE)]
            while len(x) > 1:
                x = [a + b for a, b in zip(x[::2], x[1::2])]
            out[ids[2 + layer], t] = x[0]


def finish_kernel(got, out):
    for t in range(TILES):
        out[:, 128 * t:128 * (t + 1)] = got[t // 2, t % 2] + got[PLANE + t // 2, t % 2]


def vm():
    return pl.BlockSpec(memory_space=pltpu.VMEM)


def hbm():
    return pl.BlockSpec(memory_space=pltpu.HBM)


def in_hbm(x):
    return pltpu.with_memory_space_constraint(x, pltpu.HBM)


def sm():
    return pl.BlockSpec(memory_space=pltpu.SMEM)


def shape(*dims):
    return jax.ShapeDtypeStruct(dims, jnp.float32)


def field(rows):
    return shape(rows, 2, 128, 128)


def field_hbm(rows):
    return pltpu.HBM((rows, 2, 128, 128), jnp.float32)


def scr(*dims):
    return pltpu.VMEM(dims, jnp.float32)


def wide(rows):
    return scr(rows, 2, PAD, 128)


def call(kernel, ins, outs, scratch, mib, out_specs=None):
    return pl.pallas_call(
        kernel, out_shape=outs, in_specs=ins,
        out_specs=out_specs or jax.tree.map(lambda _: vm(), outs),
        scratch_shapes=scratch,
        compiler_params=pltpu.CompilerParams(vmem_limit_bytes=mib << 20),
        cost_estimate=pl.CostEstimate(flops=20_000_000, bytes_accessed=4 << 20, transcendentals=0),
    )


def forward_and_back(angles, depth_order, slices, cotangent):
    n_row = lax.axis_size("row")
    group = lax.axis_index("illum") // PLANE
    ids = jnp.concatenate(
        [jnp.stack([lax.axis_index("row"), group]).astype(jnp.int32), depth_order])
    groups = [list(range(g * PLANE, (g + 1) * PLANE)) for g in range(2)]

    def meet(x_e, x_o, by):
        even = [(i, i ^ by) for i in range(n_row)]
        odd = [(i, i + by) for i in range(by, n_row - by) if i & by]
        odd = odd + [(j, i) for i, j in odd]
        got_o = lax.ppermute(x_o, "row", odd)
        got_e = lax.ppermute(x_e, "row", even)
        return got_e, got_o

    def exchange(x, groups=groups):
        flat = x.reshape(-1, 128)
        flat = lax.all_to_all(flat, "illum", 0, 0, axis_index_groups=groups, tiled=True)
        return flat.reshape(x.shape)

    def rows_first(x):
        return x.reshape(8, ROWS, TILES, 128).transpose(0, 2, 1, 3).reshape(-1, 128)

    mine = slices[0].reshape(ROWS, TILES, 128).transpose(1, 0, 2)
    dealt = call(double_kernel, [hbm()], pltpu.HBM((2, TILES, ROWS, 128), jnp.float32),
                 [scr(TILES, ROWS, 128), pltpu.SemaphoreType.DMA((2,))], 2, hbm())(
                     in_hbm(mine))
    dealt = dealt.reshape(2 * PLANE, 2, ROWS, 128)
    got = exchange(dealt, None)
    own, send_e, send_o = call(
        split_kernel, [sm(), vm()], (field_hbm(8), field(4), field(4)),
        [scr(8, 2, 128, 128), pltpu.SemaphoreType.DMA], 6, (hbm(), vm(), vm()))(
            ids, rows_first(cotangent))
    cot_e, cot_o = meet(send_e, send_o, 1)
    whole = call(pick_kernel, [sm(), vm()], shape(PLANE, 2, LAYERS, ROWS, 128), [],
                 2)(ids, got)
    phases = exchange(whole).reshape(-1, 128)
    w1 = call(
        adjoint_kernel, [sm(), hbm()] + [vm()] * 2, field_hbm(8),
        [scr(8, 2, 128, 128)] * 2 + [wide(16)] * 4 + [pltpu.SemaphoreType.DMA],
        14, hbm())(ids, in_hbm(own), cot_e, cot_o)
    ph_e, ph_o = meet(phases, phases, 1)
    w_e, w_o = meet(w1, w1, 1)

    table = scr(TILES * LAYERS * ROWS, 128)
    cos_own, sin_own = call(
        phase_kernel, [vm()], (shape(LAYERS * ROWS, 128, 128),) * 2, [table] * 2,
        5)(phases)
    *kept, last_e, last_o = call(
        forward_kernel, [sm()] * 2 + [vm()] * 4,
        (shape(LAYERS * EXT, 128, 128),) * 2 + (field(8),) * 3 + (field_hbm(4),) * 2,
        [table, table, scr(2, 128, 128)] + [wide(EXT)] * 5
        + [pltpu.SemaphoreType.DMA((2,))], 20, (vm(),) * 5 + (hbm(),) * 2)(
            ids, angles, ph_e, ph_o, cos_own, sin_own)
    terms = call(
        back_kernel, [sm()] + [vm()] * 8, shape(TILES * LAYERS * ROWS, 128),
        [wide(EXT)] * 2 + [scr(16, 2, 128, 128)] + [wide(EXT)] * 3, 21)(
            ids, *kept, w1, w_e, w_o)
    parts = exchange(terms).reshape(PLANE, 2, LAYERS, ROWS, 128)
    r_e, r_o = meet(last_e, last_o, 1)
    send = call(gather_kernel, [sm(), vm()], shape(2 * PLANE, 2, ROWS, 128), [],
                2)(ids, parts)
    back = exchange(send, None)
    out = call(exit_kernel, [sm()] + [hbm()] * 2 + [vm()] * 2, shape(2048, 128),
               [wide(16)] * 4 + [scr(8, 2, 128, 128), scr(2, 4, 2, 128, 128),
                                 pltpu.SemaphoreType.DMA((2,))], 13)(
                   ids, in_hbm(last_e), in_hbm(last_o), r_e, r_o)
    grad = call(finish_kernel, [vm()], shape(ROWS, COLS), [], 2)(back)
    out = out.reshape(8, TILES, ROWS, 128).transpose(0, 2, 1, 3)
    return out.reshape(cotangent.shape), grad[None]


def solution(mesh):
    placed = (P("illum", None), P(), P("illum", "row", None), P("illum", None, "row", None))
    return jax.shard_map(
        forward_and_back,
        mesh=mesh,
        in_specs=placed,
        out_specs=(P("illum", None, "row", None), P("illum", "row", None)),
        check_vma=False,
    )
```

```python
import functools
import math

import jax
import jax.numpy as jnp
from jax import lax
from jax.experimental import pallas as pl
from jax.experimental.pallas import tpu as pltpu
from jax.sharding import PartitionSpec as P


rate_scale = 0.3
ROWS = 8
COLS = 4096
TILES = COLS // 128
LAYERS = 3
HALO = 8
EXT = ROWS + 2 * HALO
N_ROW = 8
NX = ROWS * N_ROW
PAD = 144
PLANE = 16

SIN_C = (0.9999999996397458, -0.16666666036106006, 0.00833331543673961,
         -0.00019839409893936808, 2.7469726872825416e-06, -2.3138942785856126e-08)
COS_C = (0.9999999953627682, -0.49999991881071015, 0.04166643614419552,
         -0.001388649171259302, 2.4688583708756773e-05, -2.5084304017242627e-07)


def horner(coefs, z):
    r = z * coefs[-1] + coefs[-2]
    for c in coefs[-3::-1]:
        r = r * z + c
    return r


def sincos(x):
    y = x * 0.5
    z = y * y
    s = y * horner(SIN_C, z)
    c = horner(COS_C, z)
    s2 = s + s
    return s2 * c, 1.0 - s2 * s


def chunk(j):
    return slice(8 * j, 8 * j + 8)


def padded(j, shift=0):
    return slice(8 + 8 * j + shift, 16 + 8 * j + shift)


def fill_pads(ref, rows):
    flat = ref.reshape(rows * 2 * PAD, 128)
    tile = lax.broadcasted_iota(jnp.int32, (rows * 2, 128), 1) & (TILES - 1)
    high = flat[pl.ds(135, rows * 2, stride=PAD), :]
    low = flat[pl.ds(8, rows * 2, stride=PAD), :]
    flat[pl.ds(7, rows * 2, stride=PAD), :] = jnp.where(tile == 0, 0.0, pltpu.roll(high, 1, 1))
    flat[pl.ds(136, rows * 2, stride=PAD), :] = jnp.where(
        tile == TILES - 1, 0.0, pltpu.roll(low, 127, 1))


def clear_outside(row, ref, base, rows):
    for at in (base - 1 - ROWS * row, base + NX - ROWS * row):
        @pl.when((at >= 0) & (at < rows))
        def _(at=at):
            ref[at] = jnp.zeros((2, PAD, 128), jnp.float32)


def lap_rows(src, r, n, k, j):
    v = [src[r + q, k, padded(j), :] for q in range(-1, n + 1)]
    out = []
    for q in range(n):
        side = src[r + q, k, padded(j, -1), :] + src[r + q, k, padded(j, 1), :]
        out.append((v[q] + v[q + 2]) + side - 4.0 * v[q + 1])
    return out


def step(row, src, rows, base, h, powers, factor, write):
    prev = src
    for n, dst in enumerate(powers):
        lo, count = base - h + 1 + n, ROWS + 2 * (h - 1 - n)

        def body(r, n, prev=prev, dst=dst):
            for k in range(2):
                for j in range(16):
                    for q, x in enumerate(lap_rows(prev, r, n, k, j)):
                        dst[r + q, k, padded(j), :] = x

        def four(i, _, body=body, lo=lo):
            body(lo + 4 * i, 4)
            return 0

        lax.fori_loop(0, count // 4, four, 0)
        if count % 4:
            body(lo + count - 2, 2)
        fill_pads(dst, rows)
        clear_outside(row, dst, base, rows)
        prev = dst
    l1, l2, l3 = powers
    c1, c2, c3, c4 = factor, -factor**2 / 2, -factor**3 / 6, factor**4 / 24
    lo = base - h + 4

    def last(i, _):
        r = lo + 2 * i
        for j in range(16):
            l4 = [lap_rows(l3, r, 2, k, j) for k in range(2)]
            for q in (0, 1):
                even, odd = [], []
                for k in range(2):
                    at = (r + q, k, padded(j), slice(None))
                    even.append(src[at] + (c2 * l2[at] + c4 * l4[k][q]))
                    odd.append(c1 * l1[at] + c3 * l3[at])
                write(r + q, j, even[0] - odd[1], even[1] + odd[0])
        return 0

    lax.fori_loop(0, (ROWS + 2 * (h - 4)) // 2, last, 0)


def natural(g, k, r):
    return pl.ds((g * 2 + k) * TILES * ROWS + r, TILES, stride=ROWS)


def turned(cot, k, r):
    return jnp.concatenate([cot[natural(g, k, r), :] for g in range(4)], axis=0).T


def split_kernel(ids, cot, out, send_e, send_o, held, own, sems):
    size = TILES * ROWS
    fetch = [
        pltpu.make_async_copy(
            cot.at[size * n:size * (n + 1)], held.at[size * n:size * (n + 1)], sems.at[n])
        for n in range(8)
    ]
    for k in range(2):
        for g in range(4):
            fetch[2 * g + k].start()
    for k in range(2):
        for g in range(4):
            fetch[2 * g + k].wait()

        def body(r, _, k=k):
            own[r, k] = turned(held, k, r)
            return 0

        lax.fori_loop(0, ROWS, body, 0, unroll=2)
    keep = pltpu.make_async_copy(own, out, sems.at[0])
    keep.start()
    odd = ids[0] & 1
    for r in range(4):
        send_e[r] = own[r + 4 * (1 - odd)]
        send_o[r] = own[r + 4 * odd]
    keep.wait()


def put(dst, at, src, n):
    def body(r, _):
        for k in range(2):
            dst[at + r, k, 8:136, :] = src[r, k]
        return 0

    lax.fori_loop(0, n, body, 0)


def adjoint_kernel(ids, own, got_e, got_o, out, own_v, res, u, l1, l2, l3, sem):
    row = ids[0]
    odd = row & 1
    fetch = pltpu.make_async_copy(own, own_v, sem)
    fetch.start()
    put(u, 12 - 12 * odd, got_e, 4)
    put(u, 12 * odd, got_o, 4)
    fetch.wait()
    put(u, 4, own_v, 8)
    fill_pads(u, 16)

    def write(r, j, re, im):
        res[r - 4, 0, chunk(j), :] = re
        res[r - 4, 1, chunk(j), :] = im

    step(row, u, 16, 4, 4, (l1, l2, l3), -rate_scale, write)
    give = pltpu.make_async_copy(res, out, sem)
    give.start()
    give.wait()


def exit_kernel(ids, sent_e, sent_o, got_e, got_o, out, u, l1, l2, l3, res, held, sems):
    row = ids[0]
    odd = row & 1
    fetch = [
        pltpu.make_async_copy(src, held.at[n], sems.at[n])
        for n, src in enumerate((sent_e, sent_o))
    ]
    for c in fetch:
        c.start()
    put(u, 12 - 12 * odd, got_e, 4)
    put(u, 12 * odd, got_o, 4)
    fetch[0].wait()
    put(u, 8 - 4 * odd, held.at[0], 4)
    fetch[1].wait()
    put(u, 4 + 4 * odd, held.at[1], 4)
    fill_pads(u, 16)

    def write(r, j, re, im):
        res[r - 4, 0, chunk(j), :] = re
        res[r - 4, 1, chunk(j), :] = im

    step(row, u, 16, 4, 4, (l1, l2, l3), rate_scale, write)

    def body(r, _):
        for k in range(2):
            x = res[r, k].T
            for g in range(4):
                out[natural(g, k, r), :] = x[g * TILES:(g + 1) * TILES]
        return 0

    lax.fori_loop(0, ROWS, body, 0)


def trig_tables(phases, cos_n, sin_n):
    def body(i, _):
        at = pl.ds(pl.multiple_of(i * 96, 8), 96)
        s, c = sincos(phases[at, :])
        sin_n[at, :] = s
        cos_n[at, :] = c
        return 0

    lax.fori_loop(0, TILES // 4, body, 0)


def spread(ref, n):
    x = ref[pl.ds(n, TILES, stride=LAYERS * ROWS), :]
    return jnp.concatenate([x] * 4, axis=0).T


def phase_kernel(phases, cos_out, sin_out, cos_n, sin_n):
    trig_tables(phases, cos_n, sin_n)

    def body(i, _):
        for q in range(4):
            n = 4 * i + q
            cos_out[n] = spread(cos_n, n)
            sin_out[n] = spread(sin_n, n)
        return 0

    lax.fori_loop(0, LAYERS * ROWS // 4, body, 0)


def forward_kernel(ids, angles, ph_e, ph_o, cos_own, sin_own,
                   cosr, sinr, keep0, keep1, keep2, last_e, last_o,
                   cos_n, sin_n, beam, u, v, l1, l2, l3, sems):
    row = ids[0]
    odd = row & 1
    for ph, above in ((ph_e, odd), (ph_o, 1 - odd)):
        trig_tables(ph, cos_n, sin_n)
        first = (HALO + ROWS) * (1 - above)
        for layer in range(LAYERS):
            lo, count = (4 * above, 4) if layer == 1 else (0, 8)

            def body(i, _, layer=layer, first=first, lo=lo):
                for q in range(4):
                    r = lo + 4 * i + q
                    cosr[layer * EXT + first + r] = spread(cos_n, layer * ROWS + r)
                    sinr[layer * EXT + first + r] = spread(sin_n, layer * ROWS + r)
                return 0

            lax.fori_loop(0, count // 4, body, 0)
    for layer in range(LAYERS):
        def copy(r, _, layer=layer):
            cosr[layer * EXT + HALO + r] = cos_own[layer * ROWS + r]
            sinr[layer * EXT + HALO + r] = sin_own[layer * ROWS + r]
            return 0

        lax.fori_loop(0, ROWS, copy, 0)

    lane = lax.broadcasted_iota(jnp.int32, (8, 128), 1)
    sub = lax.broadcasted_iota(jnp.int32, (8, 128), 0)
    beam_of = lane >> 5
    pv, qv = [
        jnp.where(beam_of < 2,
                  jnp.where(beam_of == 0, angles[0, n], angles[1, n]),
                  jnp.where(beam_of == 2, angles[2, n], angles[3, n]))
        for n in range(2)
    ]
    for j in range(16):
        col = (lane & (TILES - 1)) * 128 + sub + 8 * j
        k = (qv * col) & (COLS - 1)
        s, c = sincos((k - COLS // 2).astype(jnp.float32) * (2.0 * math.pi / COLS))
        beam[0, chunk(j), :] = -c
        beam[1, chunk(j), :] = -s

    phase_at = functools.partial(rotation, cosr, sinr)

    def incident(i, _):
        for r in (2 * i, 2 * i + 1):
            k = (pv * (row * ROWS + r - HALO)) & (NX - 1)
            sa, ca = sincos((k - NX // 2).astype(jnp.float32) * (2.0 * math.pi / NX))
            for j in range(16):
                c, s = phase_at(0, r, j)
                a = sa * s - ca * c
                b = -(sa * c + ca * s)
                er, ei = beam[0, chunk(j), :], beam[1, chunk(j), :]
                u[r, 0, padded(j), :] = er * a - ei * b
                u[r, 1, padded(j), :] = ei * a + er * b
        return 0

    lax.fori_loop(0, EXT // 2, incident, 0)
    fill_pads(u, EXT)
    clear_outside(row, u, HALO, EXT)

    def write_v(r, j, re, im):
        c, s = phase_at(1, r, j)
        v[r, 0, padded(j), :] = re * c - im * s
        v[r, 1, padded(j), :] = re * s + im * c

    step(row, u, EXT, HALO, 8, (l1, l2, l3), rate_scale, write_v)
    fill_pads(v, EXT)
    clear_outside(row, v, HALO, EXT)

    def write_last(r, j, re, im):
        c, s = phase_at(2, r, j)
        keep2[r - HALO, 0, chunk(j), :] = re * c - im * s
        keep2[r - HALO, 1, chunk(j), :] = re * s + im * c

    step(row, v, EXT, HALO, 4, (l1, l2, l3), rate_scale, write_last)
    give = [
        pltpu.make_async_copy(keep2.at[pl.ds(at, 4)], dst, sems.at[n])
        for n, (at, dst) in enumerate(((4 * (1 - odd), last_e), (4 * odd, last_o)))
    ]
    for c in give:
        c.start()

    def keep(r, _):
        for k in range(2):
            keep0[r, k] = u[HALO + r, k, 8:136, :]
            keep1[r, k] = v[HALO + r, k, 8:136, :]
        return 0

    lax.fori_loop(0, ROWS, keep, 0)
    for c in give:
        c.wait()


def rotation(cosr, sinr, layer, r, j):
    return cosr[layer * EXT + r, chunk(j), :], sinr[layer * EXT + r, chunk(j), :]


def back_kernel(ids, cosr, sinr, keep0, keep1, keep2, w1, w_e, w_o, terms,
                w, w2, raw, l1, l2, l3):
    row = ids[0]
    odd = row & 1
    phase_at = functools.partial(rotation, cosr, sinr)

    def term(layer, adjoint, stored):
        def body(i, _):
            for r in (4 * i, 4 * i + 1, 4 * i + 2, 4 * i + 3):
                x = adjoint(r, 1) * stored(r, 0) - adjoint(r, 0) * stored(r, 1)
                x = x.T
                x = (x[:TILES] + x[TILES:2 * TILES]) + (x[2 * TILES:3 * TILES] + x[3 * TILES:])
                terms[pl.ds(layer * ROWS + r, TILES, stride=LAYERS * ROWS), :] = x
            return 0

        lax.fori_loop(0, ROWS // 4, body, 0)

    def of(ref, at=0):
        return lambda r, k: ref[at + r, k]

    for src, at in ((w1, HALO), (w_e, 16 - 16 * odd), (w_o, 16 * odd)):
        def back(r, _, src=src, at=at):
            for j in range(16):
                c, s = phase_at(2, at + r, j)
                re, im = src[r, 0, chunk(j), :], src[r, 1, chunk(j), :]
                w[at + r, 0, padded(j), :] = re * c + im * s
                w[at + r, 1, padded(j), :] = im * c - re * s
            return 0

        lax.fori_loop(0, ROWS, back, 0)
    term(2, of(w1), of(keep2))
    fill_pads(w, EXT)
    clear_outside(row, w, HALO, EXT)

    def mid(r, j, re, im):
        c, s = phase_at(1, r, j)
        raw[r - 4, 0, chunk(j), :] = re
        raw[r - 4, 1, chunk(j), :] = im
        w2[r, 0, padded(j), :] = re * c + im * s
        w2[r, 1, padded(j), :] = im * c - re * s

    step(row, w, EXT, HALO, 8, (l1, l2, l3), -rate_scale, mid)
    fill_pads(w2, EXT)
    clear_outside(row, w2, HALO, EXT)
    term(1, of(raw, 4), of(keep1))

    def final(r, j, re, im):
        raw[r - 4, 0, chunk(j), :] = re
        raw[r - 4, 1, chunk(j), :] = im

    step(row, w2, EXT, HALO, 4, (l1, l2, l3), -rate_scale, final)
    term(0, of(raw, 4), of(keep0))


def double_kernel(mine, out, held, sems):
    fetch = pltpu.make_async_copy(mine, held, sems.at[0])
    fetch.start()
    fetch.wait()
    give = [pltpu.make_async_copy(held, out.at[n], sems.at[n]) for n in range(2)]
    for c in give:
        c.start()
    for c in give:
        c.wait()


def pick_kernel(ids, got, out):
    for layer in range(LAYERS):
        for t in range(2):
            x = got[ids[2 + layer], t]
            for d in range(PLANE):
                out[d, t, layer] = x


def gather_kernel(ids, parts, out):
    out[...] = jnp.zeros_like(out)
    for layer in range(LAYERS):
        for t in range(2):
            x = [parts[d, t, layer] for d in range(PLANE)]
            while len(x) > 1:
                x = [a + b for a, b in zip(x[::2], x[1::2])]
            out[ids[2 + layer], t] = x[0]


def finish_kernel(got, out):
    for t in range(TILES):
        out[:, 128 * t:128 * (t + 1)] = got[t // 2, t % 2] + got[PLANE + t // 2, t % 2]


def vm():
    return pl.BlockSpec(memory_space=pltpu.VMEM)


def hbm():
    return pl.BlockSpec(memory_space=pltpu.HBM)


def in_hbm(x):
    return pltpu.with_memory_space_constraint(x, pltpu.HBM)


def sm():
    return pl.BlockSpec(memory_space=pltpu.SMEM)


def shape(*dims):
    return jax.ShapeDtypeStruct(dims, jnp.float32)


def field(rows):
    return shape(rows, 2, 128, 128)


def field_hbm(rows):
    return pltpu.HBM((rows, 2, 128, 128), jnp.float32)


def scr(*dims):
    return pltpu.VMEM(dims, jnp.float32)


def wide(rows):
    return scr(rows, 2, PAD, 128)


def call(kernel, ins, outs, scratch, mib, out_specs=None):
    return pl.pallas_call(
        kernel, out_shape=outs, in_specs=ins,
        out_specs=out_specs or jax.tree.map(lambda _: vm(), outs),
        scratch_shapes=scratch,
        compiler_params=pltpu.CompilerParams(vmem_limit_bytes=mib << 20),
        cost_estimate=pl.CostEstimate(flops=20_000_000, bytes_accessed=4 << 20, transcendentals=0),
    )


def forward_and_back(angles, depth_order, slices, cotangent):
    n_row = lax.axis_size("row")
    group = lax.axis_index("illum") // PLANE
    ids = jnp.concatenate(
        [jnp.stack([lax.axis_index("row"), group]).astype(jnp.int32), depth_order])
    groups = [list(range(g * PLANE, (g + 1) * PLANE)) for g in range(2)]

    def meet(x_e, x_o, by):
        even = [(i, i ^ by) for i in range(n_row)]
        odd = [(i, i + by) for i in range(by, n_row - by) if i & by]
        odd = odd + [(j, i) for i, j in odd]
        got_o = lax.ppermute(x_o, "row", odd)
        got_e = lax.ppermute(x_e, "row", even)
        return got_e, got_o

    def exchange(x, groups=groups):
        flat = x.reshape(-1, 128)
        flat = lax.all_to_all(flat, "illum", 0, 0, axis_index_groups=groups, tiled=True)
        return flat.reshape(x.shape)

    def rows_first(x):
        return x.reshape(8, ROWS, TILES, 128).transpose(0, 2, 1, 3).reshape(-1, 128)

    mine = slices[0].reshape(ROWS, TILES, 128).transpose(1, 0, 2)
    dealt = call(double_kernel, [hbm()], pltpu.HBM((2, TILES, ROWS, 128), jnp.float32),
                 [scr(TILES, ROWS, 128), pltpu.SemaphoreType.DMA((2,))], 2, hbm())(
                     in_hbm(mine))
    dealt = dealt.reshape(2 * PLANE, 2, ROWS, 128)
    got = exchange(dealt, None)
    own, send_e, send_o = call(
        split_kernel, [sm(), hbm()], (field_hbm(8), field(4), field(4)),
        [scr(2048, 128), scr(8, 2, 128, 128), pltpu.SemaphoreType.DMA((8,))], 6,
        (hbm(), vm(), vm()))(ids, in_hbm(rows_first(cotangent)))
    cot_e, cot_o = meet(send_e, send_o, 1)
    whole = call(pick_kernel, [sm(), vm()], shape(PLANE, 2, LAYERS, ROWS, 128), [],
                 2)(ids, got)
    phases = exchange(whole).reshape(-1, 128)
    w1 = call(
        adjoint_kernel, [sm(), hbm()] + [vm()] * 2, field_hbm(8),
        [scr(8, 2, 128, 128)] * 2 + [wide(16)] * 4 + [pltpu.SemaphoreType.DMA],
        14, hbm())(ids, in_hbm(own), cot_e, cot_o)
    ph_e, ph_o = meet(phases, phases, 1)
    w_e, w_o = meet(w1, w1, 1)

    table = scr(TILES * LAYERS * ROWS, 128)
    cos_own, sin_own = call(
        phase_kernel, [vm()], (shape(LAYERS * ROWS, 128, 128),) * 2, [table] * 2,
        5)(phases)
    *kept, last_e, last_o = call(
        forward_kernel, [sm()] * 2 + [vm()] * 4,
        (shape(LAYERS * EXT, 128, 128),) * 2 + (field(8),) * 3 + (field_hbm(4),) * 2,
        [table, table, scr(2, 128, 128)] + [wide(EXT)] * 5
        + [pltpu.SemaphoreType.DMA((2,))], 20, (vm(),) * 5 + (hbm(),) * 2)(
            ids, angles, ph_e, ph_o, cos_own, sin_own)
    terms = call(
        back_kernel, [sm()] + [vm()] * 8, shape(TILES * LAYERS * ROWS, 128),
        [wide(EXT)] * 2 + [scr(16, 2, 128, 128)] + [wide(EXT)] * 3, 21)(
            ids, *kept, w1, w_e, w_o)
    parts = exchange(terms).reshape(PLANE, 2, LAYERS, ROWS, 128)
    r_e, r_o = meet(last_e, last_o, 1)
    send = call(gather_kernel, [sm(), vm()], shape(2 * PLANE, 2, ROWS, 128), [],
                2)(ids, parts)
    back = exchange(send, None)
    out = call(exit_kernel, [sm()] + [hbm()] * 2 + [vm()] * 2, shape(2048, 128),
               [wide(16)] * 4 + [scr(8, 2, 128, 128), scr(2, 4, 2, 128, 128),
                                 pltpu.SemaphoreType.DMA((2,))], 13)(
                   ids, in_hbm(last_e), in_hbm(last_o), r_e, r_o)
    grad = call(finish_kernel, [vm()], shape(ROWS, COLS), [], 2)(back)
    out = out.reshape(8, TILES, ROWS, 128).transpose(0, 2, 1, 3)
    return out.reshape(cotangent.shape), grad[None]


def solution(mesh):
    placed = (P("illum", None), P(), P("illum", "row", None), P("illum", None, "row", None))
    return jax.shard_map(
        forward_and_back,
        mesh=mesh,
        in_specs=placed,
        out_specs=(P("illum", None, "row", None), P("illum", "row", None)),
        check_vma=False,
    )
```

```python
import functools
import math

import jax
import jax.numpy as jnp
from jax import lax
from jax.experimental import pallas as pl
from jax.experimental.pallas import tpu as pltpu
from jax.sharding import PartitionSpec as P


rate_scale = 0.3
ROWS = 8
COLS = 4096
TILES = COLS // 128
LAYERS = 3
HALO = 8
EXT = ROWS + 2 * HALO
N_ROW = 8
NX = ROWS * N_ROW
PAD = 144
PLANE = 16

SIN_C = (0.9999999996397458, -0.16666666036106006, 0.00833331543673961,
         -0.00019839409893936808, 2.7469726872825416e-06, -2.3138942785856126e-08)
COS_C = (0.9999999953627682, -0.49999991881071015, 0.04166643614419552,
         -0.001388649171259302, 2.4688583708756773e-05, -2.5084304017242627e-07)


def horner(coefs, z):
    r = z * coefs[-1] + coefs[-2]
    for c in coefs[-3::-1]:
        r = r * z + c
    return r


def sincos(x):
    y = x * 0.5
    z = y * y
    s = y * horner(SIN_C, z)
    c = horner(COS_C, z)
    s2 = s + s
    return s2 * c, 1.0 - s2 * s


def chunk(j):
    return slice(8 * j, 8 * j + 8)


def padded(j, shift=0):
    return slice(8 + 8 * j + shift, 16 + 8 * j + shift)


def fill_pads(ref, rows):
    flat = ref.reshape(rows * 2 * PAD, 128)
    tile = lax.broadcasted_iota(jnp.int32, (rows * 2, 128), 1) & (TILES - 1)
    high = flat[pl.ds(135, rows * 2, stride=PAD), :]
    low = flat[pl.ds(8, rows * 2, stride=PAD), :]
    flat[pl.ds(7, rows * 2, stride=PAD), :] = jnp.where(tile == 0, 0.0, pltpu.roll(high, 1, 1))
    flat[pl.ds(136, rows * 2, stride=PAD), :] = jnp.where(
        tile == TILES - 1, 0.0, pltpu.roll(low, 127, 1))


def clear_outside(row, ref, base, rows):
    for at in (base - 1 - ROWS * row, base + NX - ROWS * row):
        @pl.when((at >= 0) & (at < rows))
        def _(at=at):
            ref[at] = jnp.zeros((2, PAD, 128), jnp.float32)


def lap_rows(src, r, n, k, j):
    v = [src[r + q, k, padded(j), :] for q in range(-1, n + 1)]
    out = []
    for q in range(n):
        side = src[r + q, k, padded(j, -1), :] + src[r + q, k, padded(j, 1), :]
        out.append((v[q] + v[q + 2]) + side - 4.0 * v[q + 1])
    return out


def step(row, src, rows, base, h, powers, factor, write):
    prev = src
    for n, dst in enumerate(powers):
        lo, count = base - h + 1 + n, ROWS + 2 * (h - 1 - n)

        def body(r, n, prev=prev, dst=dst):
            for k in range(2):
                for j in range(16):
                    for q, x in enumerate(lap_rows(prev, r, n, k, j)):
                        dst[r + q, k, padded(j), :] = x

        def four(i, _, body=body, lo=lo):
            body(lo + 4 * i, 4)
            return 0

        lax.fori_loop(0, count // 4, four, 0)
        if count % 4:
            body(lo + count - 2, 2)
        fill_pads(dst, rows)
        clear_outside(row, dst, base, rows)
        prev = dst
    l1, l2, l3 = powers
    c1, c2, c3, c4 = factor, -factor**2 / 2, -factor**3 / 6, factor**4 / 24
    lo = base - h + 4

    def last(i, _):
        r = lo + 2 * i
        for j in range(16):
            l4 = [lap_rows(l3, r, 2, k, j) for k in range(2)]
            for q in (0, 1):
                even, odd = [], []
                for k in range(2):
                    at = (r + q, k, padded(j), slice(None))
                    even.append(src[at] + (c2 * l2[at] + c4 * l4[k][q]))
                    odd.append(c1 * l1[at] + c3 * l3[at])
                write(r + q, j, even[0] - odd[1], even[1] + odd[0])
        return 0

    lax.fori_loop(0, (ROWS + 2 * (h - 4)) // 2, last, 0)


def natural(g, k, r):
    return pl.ds((g * 2 + k) * TILES * ROWS + r, TILES, stride=ROWS)


def turned(cot, k, r):
    return jnp.concatenate([cot[natural(g, k, r), :] for g in range(4)], axis=0).T


def split_kernel(ids, cot, out, send_e, send_o, held, own, sems):
    size = TILES * ROWS
    fetch = [
        pltpu.make_async_copy(
            cot.at[size * n:size * (n + 1)], held.at[size * n:size * (n + 1)], sems.at[n])
        for n in range(8)
    ]
    for k in range(2):
        for g in range(4):
            fetch[2 * g + k].start()
    for k in range(2):
        for g in range(4):
            fetch[2 * g + k].wait()

        def body(r, _, k=k):
            own[r, k] = turned(held, k, r)
            return 0

        lax.fori_loop(0, ROWS, body, 0, unroll=2)
    keep = pltpu.make_async_copy(own, out, sems.at[0])
    keep.start()
    odd = ids[0] & 1
    for r in range(4):
        send_e[r] = own[r + 4 * (1 - odd)]
        send_o[r] = own[r + 4 * odd]
    keep.wait()


def put(dst, at, src, n):
    def body(r, _):
        for k in range(2):
            dst[at + r, k, 8:136, :] = src[r, k]
        return 0

    lax.fori_loop(0, n, body, 0, unroll=2)


def adjoint_kernel(ids, own, got_e, got_o, out, own_v, res, u, l1, l2, l3, sem):
    row = ids[0]
    odd = row & 1
    fetch = pltpu.make_async_copy(own, own_v, sem)
    fetch.start()
    put(u, 12 - 12 * odd, got_e, 4)
    put(u, 12 * odd, got_o, 4)
    fetch.wait()
    put(u, 4, own_v, 8)
    fill_pads(u, 16)

    def write(r, j, re, im):
        res[r - 4, 0, chunk(j), :] = re
        res[r - 4, 1, chunk(j), :] = im

    step(row, u, 16, 4, 4, (l1, l2, l3), -rate_scale, write)
    give = pltpu.make_async_copy(res, out, sem)
    give.start()
    give.wait()


def exit_kernel(ids, sent_e, sent_o, got_e, got_o, out, u, l1, l2, l3, res, held, flat, sems):
    row = ids[0]
    odd = row & 1
    fetch = [
        pltpu.make_async_copy(src, held.at[n], sems.at[n])
        for n, src in enumerate((sent_e, sent_o))
    ]
    for c in fetch:
        c.start()
    put(u, 12 - 12 * odd, got_e, 4)
    put(u, 12 * odd, got_o, 4)
    fetch[0].wait()
    put(u, 8 - 4 * odd, held.at[0], 4)
    fetch[1].wait()
    put(u, 4 + 4 * odd, held.at[1], 4)
    fill_pads(u, 16)

    def write(r, j, re, im):
        res[r - 4, 0, chunk(j), :] = re
        res[r - 4, 1, chunk(j), :] = im

    step(row, u, 16, 4, 4, (l1, l2, l3), rate_scale, write)

    size = TILES * ROWS
    give = [
        pltpu.make_async_copy(
            flat.at[size * n:size * (n + 1)], out.at[size * n:size * (n + 1)], sems.at[n])
        for n in range(8)
    ]
    for k in range(2):
        def body(r, _, k=k):
            x = res[r, k].T
            for g in range(4):
                flat[natural(g, k, r), :] = x[g * TILES:(g + 1) * TILES]
            return 0

        lax.fori_loop(0, ROWS, body, 0, unroll=2)
        for g in range(4):
            give[2 * g + k].start()
    for c in give:
        c.wait()


def trig_tables(phases, cos_n, sin_n):
    def body(i, _):
        at = pl.ds(pl.multiple_of(i * 96, 8), 96)
        s, c = sincos(phases[at, :])
        sin_n[at, :] = s
        cos_n[at, :] = c
        return 0

    lax.fori_loop(0, TILES // 4, body, 0)


def spread(ref, n):
    x = ref[pl.ds(n, TILES, stride=LAYERS * ROWS), :]
    return jnp.concatenate([x] * 4, axis=0).T


def phase_kernel(phases, cos_out, sin_out, cos_n, sin_n):
    trig_tables(phases, cos_n, sin_n)

    def body(i, _):
        for q in range(4):
            n = 4 * i + q
            cos_out[n] = spread(cos_n, n)
            sin_out[n] = spread(sin_n, n)
        return 0

    lax.fori_loop(0, LAYERS * ROWS // 4, body, 0)


def forward_kernel(ids, angles, ph_e, ph_o, cos_own, sin_own,
                   cosr, sinr, keep0, keep1, keep2, last_e, last_o,
                   cos_n, sin_n, beam, u, v, l1, l2, l3, sems):
    row = ids[0]
    odd = row & 1
    for ph, above in ((ph_e, odd), (ph_o, 1 - odd)):
        trig_tables(ph, cos_n, sin_n)
        first = (HALO + ROWS) * (1 - above)
        for layer in range(LAYERS):
            lo, count = (4 * above, 4) if layer == 1 else (0, 8)

            def body(i, _, layer=layer, first=first, lo=lo):
                for q in range(4):
                    r = lo + 4 * i + q
                    cosr[layer * EXT + first + r] = spread(cos_n, layer * ROWS + r)
                    sinr[layer * EXT + first + r] = spread(sin_n, layer * ROWS + r)
                return 0

            lax.fori_loop(0, count // 4, body, 0)
    for layer in range(LAYERS):
        def copy(r, _, layer=layer):
            cosr[layer * EXT + HALO + r] = cos_own[layer * ROWS + r]
            sinr[layer * EXT + HALO + r] = sin_own[layer * ROWS + r]
            return 0

        lax.fori_loop(0, ROWS, copy, 0, unroll=2)

    lane = lax.broadcasted_iota(jnp.int32, (8, 128), 1)
    sub = lax.broadcasted_iota(jnp.int32, (8, 128), 0)
    beam_of = lane >> 5
    pv, qv = [
        jnp.where(beam_of < 2,
                  jnp.where(beam_of == 0, angles[0, n], angles[1, n]),
                  jnp.where(beam_of == 2, angles[2, n], angles[3, n]))
        for n in range(2)
    ]
    for j in range(16):
        col = (lane & (TILES - 1)) * 128 + sub + 8 * j
        k = (qv * col) & (COLS - 1)
        s, c = sincos((k - COLS // 2).astype(jnp.float32) * (2.0 * math.pi / COLS))
        beam[0, chunk(j), :] = -c
        beam[1, chunk(j), :] = -s

    phase_at = functools.partial(rotation, cosr, sinr)

    def incident(i, _):
        for r in (2 * i, 2 * i + 1):
            k = (pv * (row * ROWS + r - HALO)) & (NX - 1)
            sa, ca = sincos((k - NX // 2).astype(jnp.float32) * (2.0 * math.pi / NX))
            for j in range(16):
                c, s = phase_at(0, r, j)
                a = sa * s - ca * c
                b = -(sa * c + ca * s)
                er, ei = beam[0, chunk(j), :], beam[1, chunk(j), :]
                u[r, 0, padded(j), :] = er * a - ei * b
                u[r, 1, padded(j), :] = ei * a + er * b
        return 0

    lax.fori_loop(0, EXT // 2, incident, 0)
    fill_pads(u, EXT)
    clear_outside(row, u, HALO, EXT)

    def write_v(r, j, re, im):
        c, s = phase_at(1, r, j)
        v[r, 0, padded(j), :] = re * c - im * s
        v[r, 1, padded(j), :] = re * s + im * c

    step(row, u, EXT, HALO, 8, (l1, l2, l3), rate_scale, write_v)
    fill_pads(v, EXT)
    clear_outside(row, v, HALO, EXT)

    def write_last(r, j, re, im):
        c, s = phase_at(2, r, j)
        keep2[r - HALO, 0, chunk(j), :] = re * c - im * s
        keep2[r - HALO, 1, chunk(j), :] = re * s + im * c

    step(row, v, EXT, HALO, 4, (l1, l2, l3), rate_scale, write_last)
    give = [
        pltpu.make_async_copy(keep2.at[pl.ds(at, 4)], dst, sems.at[n])
        for n, (at, dst) in enumerate(((4 * (1 - odd), last_e), (4 * odd, last_o)))
    ]
    for c in give:
        c.start()

    def keep(r, _):
        for k in range(2):
            keep0[r, k] = u[HALO + r, k, 8:136, :]
            keep1[r, k] = v[HALO + r, k, 8:136, :]
        return 0

    lax.fori_loop(0, ROWS, keep, 0, unroll=2)
    for c in give:
        c.wait()


def rotation(cosr, sinr, layer, r, j):
    return cosr[layer * EXT + r, chunk(j), :], sinr[layer * EXT + r, chunk(j), :]


def back_kernel(ids, cosr, sinr, keep0, keep1, keep2, w1, w_e, w_o, terms,
                w, w2, raw, l1, l2, l3):
    row = ids[0]
    odd = row & 1
    phase_at = functools.partial(rotation, cosr, sinr)

    def term(layer, adjoint, stored):
        def body(i, _):
            for r in (4 * i, 4 * i + 1, 4 * i + 2, 4 * i + 3):
                x = adjoint(r, 1) * stored(r, 0) - adjoint(r, 0) * stored(r, 1)
                x = x.T
                x = (x[:TILES] + x[TILES:2 * TILES]) + (x[2 * TILES:3 * TILES] + x[3 * TILES:])
                terms[pl.ds(layer * ROWS + r, TILES, stride=LAYERS * ROWS), :] = x
            return 0

        lax.fori_loop(0, ROWS // 4, body, 0)

    def of(ref, at=0):
        return lambda r, k: ref[at + r, k]

    for src, at in ((w1, HALO), (w_e, 16 - 16 * odd), (w_o, 16 * odd)):
        def back(r, _, src=src, at=at):
            for j in range(16):
                c, s = phase_at(2, at + r, j)
                re, im = src[r, 0, chunk(j), :], src[r, 1, chunk(j), :]
                w[at + r, 0, padded(j), :] = re * c + im * s
                w[at + r, 1, padded(j), :] = im * c - re * s
            return 0

        lax.fori_loop(0, ROWS, back, 0, unroll=2)
    term(2, of(w1), of(keep2))
    fill_pads(w, EXT)
    clear_outside(row, w, HALO, EXT)

    def mid(r, j, re, im):
        c, s = phase_at(1, r, j)
        raw[r - 4, 0, chunk(j), :] = re
        raw[r - 4, 1, chunk(j), :] = im
        w2[r, 0, padded(j), :] = re * c + im * s
        w2[r, 1, padded(j), :] = im * c - re * s

    step(row, w, EXT, HALO, 8, (l1, l2, l3), -rate_scale, mid)
    fill_pads(w2, EXT)
    clear_outside(row, w2, HALO, EXT)
    term(1, of(raw, 4), of(keep1))

    def final(r, j, re, im):
        raw[r - 4, 0, chunk(j), :] = re
        raw[r - 4, 1, chunk(j), :] = im

    step(row, w2, EXT, HALO, 4, (l1, l2, l3), -rate_scale, final)
    term(0, of(raw, 4), of(keep0))


def double_kernel(mine, out, held, sems):
    fetch = pltpu.make_async_copy(mine, held, sems.at[0])
    fetch.start()
    fetch.wait()
    give = [pltpu.make_async_copy(held, out.at[n], sems.at[n]) for n in range(2)]
    for c in give:
        c.start()
    for c in give:
        c.wait()


def pick_kernel(ids, got, out):
    for layer in range(LAYERS):
        for t in range(2):
            x = got[ids[2 + layer], t]
            for d in range(PLANE):
                out[d, t, layer] = x


def gather_kernel(ids, parts, out):
    out[...] = jnp.zeros_like(out)
    for layer in range(LAYERS):
        for t in range(2):
            x = [parts[d, t, layer] for d in range(PLANE)]
            while len(x) > 1:
                x = [a + b for a, b in zip(x[::2], x[1::2])]
            out[ids[2 + layer], t] = x[0]


def finish_kernel(got, out):
    for t in range(TILES):
        out[:, 128 * t:128 * (t + 1)] = got[t // 2, t % 2] + got[PLANE + t // 2, t % 2]


def vm():
    return pl.BlockSpec(memory_space=pltpu.VMEM)


def hbm():
    return pl.BlockSpec(memory_space=pltpu.HBM)


def in_hbm(x):
    return pltpu.with_memory_space_constraint(x, pltpu.HBM)


def sm():
    return pl.BlockSpec(memory_space=pltpu.SMEM)


def shape(*dims):
    return jax.ShapeDtypeStruct(dims, jnp.float32)


def field(rows):
    return shape(rows, 2, 128, 128)


def field_hbm(rows):
    return pltpu.HBM((rows, 2, 128, 128), jnp.float32)


def scr(*dims):
    return pltpu.VMEM(dims, jnp.float32)


def wide(rows):
    return scr(rows, 2, PAD, 128)


def call(kernel, ins, outs, scratch, mib, out_specs=None):
    return pl.pallas_call(
        kernel, out_shape=outs, in_specs=ins,
        out_specs=out_specs or jax.tree.map(lambda _: vm(), outs),
        scratch_shapes=scratch,
        compiler_params=pltpu.CompilerParams(vmem_limit_bytes=mib << 20),
        cost_estimate=pl.CostEstimate(flops=20_000_000, bytes_accessed=4 << 20, transcendentals=0),
    )


def forward_and_back(angles, depth_order, slices, cotangent):
    n_row = lax.axis_size("row")
    group = lax.axis_index("illum") // PLANE
    ids = jnp.concatenate(
        [jnp.stack([lax.axis_index("row"), group]).astype(jnp.int32), depth_order])
    groups = [list(range(g * PLANE, (g + 1) * PLANE)) for g in range(2)]

    def meet(x_e, x_o, by):
        even = [(i, i ^ by) for i in range(n_row)]
        odd = [(i, i + by) for i in range(by, n_row - by) if i & by]
        odd = odd + [(j, i) for i, j in odd]
        got_o = lax.ppermute(x_o, "row", odd)
        got_e = lax.ppermute(x_e, "row", even)
        return got_e, got_o

    def exchange(x, groups=groups):
        flat = x.reshape(-1, 128)
        flat = lax.all_to_all(flat, "illum", 0, 0, axis_index_groups=groups, tiled=True)
        return flat.reshape(x.shape)

    def rows_first(x):
        return x.reshape(8, ROWS, TILES, 128).transpose(0, 2, 1, 3).reshape(-1, 128)

    mine = slices[0].reshape(ROWS, TILES, 128).transpose(1, 0, 2)
    dealt = call(double_kernel, [hbm()], pltpu.HBM((2, TILES, ROWS, 128), jnp.float32),
                 [scr(TILES, ROWS, 128), pltpu.SemaphoreType.DMA((2,))], 2, hbm())(
                     in_hbm(mine))
    dealt = dealt.reshape(2 * PLANE, 2, ROWS, 128)
    got = exchange(dealt, None)
    own, send_e, send_o = call(
        split_kernel, [sm(), hbm()], (field_hbm(8), field(4), field(4)),
        [scr(2048, 128), scr(8, 2, 128, 128), pltpu.SemaphoreType.DMA((8,))], 6,
        (hbm(), vm(), vm()))(ids, in_hbm(rows_first(cotangent)))
    cot_e, cot_o = meet(send_e, send_o, 1)
    whole = call(pick_kernel, [sm(), vm()], shape(PLANE, 2, LAYERS, ROWS, 128), [],
                 2)(ids, got)
    phases = exchange(whole).reshape(-1, 128)
    w1 = call(
        adjoint_kernel, [sm(), hbm()] + [vm()] * 2, field_hbm(8),
        [scr(8, 2, 128, 128)] * 2 + [wide(16)] * 4 + [pltpu.SemaphoreType.DMA],
        14, hbm())(ids, in_hbm(own), cot_e, cot_o)
    ph_e, ph_o = meet(phases, phases, 1)
    w_e, w_o = meet(w1, w1, 1)

    table = scr(TILES * LAYERS * ROWS, 128)
    cos_own, sin_own = call(
        phase_kernel, [vm()], (shape(LAYERS * ROWS, 128, 128),) * 2, [table] * 2,
        5)(phases)
    *kept, last_e, last_o = call(
        forward_kernel, [sm()] * 2 + [vm()] * 4,
        (shape(LAYERS * EXT, 128, 128),) * 2 + (field(8),) * 3 + (field_hbm(4),) * 2,
        [table, table, scr(2, 128, 128)] + [wide(EXT)] * 5
        + [pltpu.SemaphoreType.DMA((2,))], 20, (vm(),) * 5 + (hbm(),) * 2)(
            ids, angles, ph_e, ph_o, cos_own, sin_own)
    terms = call(
        back_kernel, [sm()] + [vm()] * 8, shape(TILES * LAYERS * ROWS, 128),
        [wide(EXT)] * 2 + [scr(16, 2, 128, 128)] + [wide(EXT)] * 3, 21)(
            ids, *kept, w1, w_e, w_o)
    parts = exchange(terms).reshape(PLANE, 2, LAYERS, ROWS, 128)
    r_e, r_o = meet(last_e, last_o, 1)
    send = call(gather_kernel, [sm(), vm()], shape(2 * PLANE, 2, ROWS, 128), [],
                2)(ids, parts)
    back = exchange(send, None)
    out = call(exit_kernel, [sm()] + [hbm()] * 2 + [vm()] * 2,
               pltpu.HBM((2048, 128), jnp.float32),
               [wide(16)] * 4 + [scr(8, 2, 128, 128), scr(2, 4, 2, 128, 128),
                                 scr(2048, 128), pltpu.SemaphoreType.DMA((8,))],
               14, hbm())(
                   ids, in_hbm(last_e), in_hbm(last_o), r_e, r_o)
    grad = call(finish_kernel, [vm()], shape(ROWS, COLS), [], 2)(back)
    out = out.reshape(8, TILES, ROWS, 128).transpose(0, 2, 1, 3)
    return out.reshape(cotangent.shape), grad[None]


def solution(mesh):
    placed = (P("illum", None), P(), P("illum", "row", None), P("illum", None, "row", None))
    return jax.shard_map(
        forward_and_back,
        mesh=mesh,
        in_specs=placed,
        out_specs=(P("illum", None, "row", None), P("illum", "row", None)),
        check_vma=False,
    )
```
